32 devices in a mesh: dp: 16 (over z, x, core), mp: 2 (over y).
Axes of the slice: x: 2, y: 2, z: 4, core: 2. Of those that a mesh axis runs over, the one named last changes fastest.
Arguments:
- inputs: bfloat16 [8192, 3968], P('dp', 'mp'), may hold values from -6 to 6
- grad_out: bfloat16 [8192, 2048], P('dp', 'mp'), may hold values from -0.25 to 0.25
- error: bfloat16 [32768, 3968], P(('dp', 'mp')), may hold values from -6 to 6
- q_prev: float32 [3968, 64], P('mp'), may hold values from -0.09375 to 0.09375
Outputs:
- new_error: bfloat16 [32768, 3968], P(('dp', 'mp'))
- p_basis: float32 [2048, 64], P('mp')
- q_factor: float32 [3968, 64], P('mp')
The draws below stay inside these ranges and needn't reach their ends.
All inputs are finite; a program needn't handle non-finite values.
Results may differ from the reference program's by a relative error of at most 0.0065.
Values may be sent and summed in bfloat16 or wider, within the bound.
A program may use at most 64 MiB of HBM per device.

```python
import jax
import jax.numpy as jnp
from jax import lax

D = 3968
OUT = 2048
R = 64
TOK_DEV = 512
TOKENS = 8192
ROWS = 32768
N_DP = 16


def block_scale(stream_key, dims, cuts, smallest, top_value):
    level, own = 1.0, jax.random.fold_in(stream_key, 6)
    for dim, parts in cuts:
        steps = jnp.exp(jax.random.uniform(jax.random.fold_in(own, dim), (parts,), jnp.float32, smallest / len(cuts), top_value / len(cuts)))
        level = level * jnp.repeat(steps, dims[dim] // parts).reshape([-1 if axis == dim else 1 for axis in range(len(dims))])
    return level


def noise(rng, shape, scale, limit, split=(), kind=jnp.bfloat16):
    array = jax.random.normal(rng, shape, jnp.float32) * scale
    if len(split) > 0:
        array = block_scale(rng, shape, split, -0.22, 0.18) * array
    return jnp.clip(array, min=-limit, max=limit).astype(kind)


def setup_inputs(seed: int = 0) -> dict:
    arg_keys = jax.random.split(jax.random.key(seed), 5)
    return {
        "inputs": noise(arg_keys[0], (TOKENS, D), 1.0, 6.0, ((0, 16), (1, 2))),
        "grad_out": noise(arg_keys[1], (TOKENS, OUT), TOK_DEV ** -0.5, 0.25, ((0, 16), (1, 2))),
        "error": noise(arg_keys[2], (ROWS, D), 1.0, 6.0, ((0, 32),)),
        "q_prev": noise(arg_keys[3], (D, R), D ** -0.5, 0.09375, ((0, 2),), jnp.float32),
    }


def reference(inputs, grad_out, error, q_prev):
    highest = lax.Precision.HIGHEST
    xs = inputs.reshape(N_DP, TOK_DEV, D)
    gs = grad_out.reshape(N_DP, TOK_DEV, OUT)
    es = error.reshape(N_DP, OUT, D)

    def merged(index):
        xrow = lax.dynamic_index_in_dim(xs, index, 0, False)
        grow = lax.dynamic_index_in_dim(gs, index, 0, False)
        erow = lax.dynamic_index_in_dim(es, index, 0, False)
        prod = lax.dot_general(grow.astype(jnp.float32), xrow.astype(jnp.float32), (((0,), (0,)), ((), ())), preferred_element_type=jnp.float32)
        return prod + erow.astype(jnp.float32)

    def add_p(carry, index):
        return (carry + jnp.dot(merged(index), q_prev, precision=highest), None)
    indices = jnp.arange(N_DP, dtype=jnp.int32)
    psum_all, _ = lax.scan(add_p, jnp.zeros((OUT, R), jnp.float32), indices)
    factor = psum_all / N_DP
    gram = jnp.dot(factor.T, factor, precision=highest)
    ridge = 0.01 * jnp.trace(gram) / R + 1e-06
    gram = gram + ridge * jnp.eye(R, dtype=jnp.float32)
    lower = jnp.linalg.cholesky(gram)
    p_hat = jax.scipy.linalg.solve_triangular(lower, factor.T, lower=True).T

    def add_q(carry, index):
        term = lax.dot_general(merged(index), p_hat, (((0,), (0,)), ((), ())), precision=highest)
        return (carry + term, None)
    qsum_all, _ = lax.scan(add_q, jnp.zeros((D, R), jnp.float32), indices)
    q_factor = qsum_all / N_DP
    approx = jnp.dot(p_hat, q_factor.T, precision=highest)

    def residue(index):
        return (merged(index) - approx).astype(jnp.bfloat16)
    new_error = lax.map(residue, indices).reshape(N_DP * OUT, D)
    return (new_error, p_hat * jnp.sqrt(jnp.float32(OUT)), q_factor)
```

```python
import functools

import jax
import jax.numpy as jnp
from jax import lax
from jax.experimental import pallas as pl
from jax.experimental.pallas import tpu as pltpu
from jax.sharding import PartitionSpec as P

MESH = pl.DeviceIdType.MESH
PIECE = 64
NN = (((1,), (0,)), ((), ()))
NT = (((1,), (1,)), ((), ()))
TN = (((0,), (0,)), ((), ()))
TT = (((0,), (1,)), ((), ()))
LANES = 128


def dot(a, b, dims=NN):
    return lax.dot_general(a, b, dims, preferred_element_type=jnp.float32)


def exact(a, b, dims=NN):
    return lax.dot_general(a, b, dims, precision=lax.Precision.HIGHEST, preferred_element_type=jnp.float32)


def split(value):
    head = value.astype(jnp.bfloat16)
    rest = (value - head.astype(jnp.float32)).astype(jnp.bfloat16)
    return jnp.concatenate([head, rest], axis=0)


def fold(terms):
    rank = terms.shape[0] // 2
    return terms[:rank] + terms[rank:]


def inverse_factor(gram):
    rank = gram.shape[0]
    row = lax.broadcasted_iota(jnp.int32, gram.shape, 0)
    diag = row == lax.broadcasted_iota(jnp.int32, gram.shape, 1)
    ridge = 0.01 * jnp.sum(jnp.where(diag, gram, 0.0), keepdims=True) / rank + 1e-06
    work = gram + jnp.where(diag, ridge, 0.0)
    inverse = jnp.where(diag, 1.0, 0.0)
    row1 = lax.broadcasted_iota(jnp.int32, (rank, 1), 0)
    for k in range(0, rank, 2):
        first, second = work[k : k + 1, :], work[k + 1 : k + 2, :]
        one, two = work[:, k : k + 1], work[:, k + 1 : k + 2]
        cross = first[:, k + 1 : k + 2]
        ratio = second[:, k : k + 1] / first[:, k : k + 1]
        factor = jnp.where(row1 > k, one, 0.0) / first[:, k : k + 1]
        pivot = second[:, k + 1 : k + 2] - ratio * cross
        later = jnp.where(row1 > k + 1, two - factor * cross, 0.0) / pivot
        second = second - ratio * first
        begin = inverse[k : k + 1, :]
        follow = inverse[k + 1 : k + 2, :] - ratio * begin
        inverse = inverse - factor * begin - later * follow
        work = work - factor * first - later * second
    pivots = jnp.sum(jnp.where(diag, work, 0.0), axis=1, keepdims=True)
    return inverse * lax.rsqrt(pivots)


def exchange_kernel(
    n_dp, x_hbm, g_hbm, e_hbm, q_hbm,
    merged_ref, pair_ref, basis_ref, qg_ref,
    g_ref, q_ref, e_ref, xf, qs, u_send, u_recv, v_send, v_recv, pw, p1, p2, pg, gs, qf, xt, q1, qb, q2, y1, y2,
    load_sem, x_ssem, x_rsem, ssem, rsem,
):
    dp, mp = lax.axis_index("dp"), lax.axis_index("mp")
    core, xx, zz = lax.rem(dp, 2), lax.rem(dp // 2, 2), dp // 4
    n_z = n_dp // 4
    chips = n_dp // 2
    rank, own = q_ref.shape
    n, features = merged_ref.shape
    m = qf.shape[1]

    def device(d_core, d_x, d_y, k):
        z = lax.rem(zz + k, n_z)
        c = 1 - core if d_core else core
        x = 1 - xx if d_x else xx
        return ((z * 2 + x) * 2 + c, 1 - mp if d_y else mp)

    core_mate, y_mate, cross_mate = device(1, 0, 0, 0), device(0, 0, 1, 0), device(1, 0, 1, 0)
    offsets = [(a, k) for k in range(n_z) for a in (1, 0) if (a, k) != (0, 0)]
    peers = [device(0, a, 0, k) for a, k in offsets]
    places = [lax.rem(zz + k, n_z) * 2 + (1 - xx if a else xx) for a, k in offsets]
    place = zz * 2 + xx

    x_base = pl.multiple_of(mp * own, PIECE)
    mine = pl.ds(x_base, own)
    load_x = pltpu.make_async_copy(x_hbm, xf.at[mine], load_sem.at[0])
    load_e = pltpu.make_async_copy(e_hbm, e_ref, load_sem.at[1])
    load_g = pltpu.make_async_copy(g_hbm, g_ref, load_sem.at[2])
    load_q = pltpu.make_async_copy(q_hbm, q_ref, load_sem.at[3])
    load_q.start()
    load_x.start()
    load_g.start()
    load_e.start()
    barrier = pltpu.get_barrier_semaphore()
    mates = [core_mate, y_mate, cross_mate] + peers
    for mate in mates:
        pl.semaphore_signal(barrier, inc=1, device_id=mate, device_id_type=MESH)

    sent = []

    def send(src, dst, mate):
        index = len(sent)
        copy = pltpu.make_async_remote_copy(
            src_ref=src, dst_ref=dst, send_sem=ssem.at[index], recv_sem=rsem.at[index],
            device_id=mate, device_id_type=MESH,
        )
        copy.start()
        sent.append(copy)
        return copy

    pieces = own // PIECE
    flat = own // LANES * LANES
    middle = pl.multiple_of(mp * own + (1 - mp) * flat, PIECE)
    flying = []

    def start_x(count):
        for j in range(len(flying), min(pieces, len(flying) + count)):
            row = middle if j == pieces - 1 else x_base + mp * PIECE + j * PIECE
            part = pl.ds(pl.multiple_of(row, PIECE), PIECE)
            copy = pltpu.make_async_remote_copy(
                src_ref=xf.at[part], dst_ref=xf.at[part], send_sem=x_ssem.at[j], recv_sem=x_rsem.at[j],
                device_id=y_mate, device_id_type=MESH,
            )
            copy.start()
            flying.append(copy)

    landed = [0]

    def land_x(count):
        for copy in flying[landed[0] : count]:
            copy.wait_recv()
        landed[0] = max(landed[0], count)

    def merge(begin, size):
        columns = pl.ds(pl.multiple_of(begin, LANES), size)
        product = dot(g_ref[...], xf[columns, :], TT)
        merged_ref[:, columns] = product + e_ref[:, columns].astype(jnp.float32)

    def merge_own(step):
        size = flat // 3
        merge(mp * (flat + LANES) + step * size, size)

    def merge_other(begin, end):
        land_x(end // PIECE)
        merge((1 - mp) * (flat + LANES) + begin, end - begin)

    load_q.wait()
    q_pair = split(q_ref[...])
    qs[mp] = q_pair
    pl.semaphore_wait(barrier, len(mates))
    my_half = pl.ds(pl.multiple_of(core * rank, 16), rank)
    q_copy = send(qs.at[mp, my_half], qs.at[mp, my_half], y_mate)
    load_x.wait()
    u_own = fold(dot(q_pair, xf[mine]))
    u_send[...] = u_own
    u_copy = send(u_send, u_recv, y_mate)
    start_x(STEPS[0])
    q_copy.wait_recv()
    q_pass = send(qs.at[1 - mp, my_half], qs.at[1 - mp, my_half], core_mate)
    load_g.wait()
    load_e.wait()
    merge_own(0)
    q_pass.wait_recv()
    q_all = jnp.concatenate([qs[0], qs[1]], axis=1)
    p_part = fold(dot(q_all, e_ref[...], NT))
    u_copy.wait_recv()
    pw[...] = p_part + fold(dot(split(u_own + u_recv[...]), g_ref[...]))

    def part(offset, size):
        return pl.ds(pl.multiple_of(offset, size), size)

    n1, height = n // 2, rank // chips
    b1 = part(core * n1, n1)
    level = part(place * height, height)
    copy = send(pw.at[:, part((1 - core) * n1, n1)], p1, core_mate)
    start_x(STEPS[1])
    copy.wait_recv()
    pw[:, b1] = pw[:, b1] + p1[...]
    copies = [
        send(pw.at[part(there * height, height), b1], p2.at[k], mate)
        for k, (there, mate) in enumerate(zip(places, peers))
    ]
    start_x(STEPS[2])
    merge_own(1)
    total = pw[level, b1]
    for k, copy in enumerate(copies):
        copy.wait_recv()
        total = total + p2[k]
    pg[level, b1] = total * (1.0 / n_dp)
    copies = [send(pg.at[level, b1], pg.at[level, b1], mate) for mate in peers]
    start_x(STEPS[3])
    merge_own(2)
    for copy in copies:
        copy.wait_recv()

    p_half = pg[:, b1]
    slot = mp * 2 + core
    p_pass = send(pg.at[:, b1], pg.at[:, b1], core_mate)
    gs[slot] = exact(p_half, p_half, NT)
    grams = [send(gs.at[slot], gs.at[slot], mate) for mate in (y_mate, cross_mate, core_mate)]
    p_pass.wait_recv()
    mean = pg[...]
    mean_pair = split(mean)
    v_own = fold(dot(mean_pair, g_ref[...], NT))
    v_send[...] = v_own
    v_copy = send(v_send, v_recv, y_mate)
    start_x(STEPS[4])
    qf[:, features:] = jnp.zeros((rank, m - features), jnp.float32)
    for lo in range(0, features, m // 4):
        hi = min(lo + m // 4, features)
        qf[:, lo:hi] = fold(dot(mean_pair, e_ref[:, lo:hi]))
    for copy in grams:
        copy.wait_recv()
    lower = inverse_factor(gs[0] + gs[1] + gs[2] + gs[3])

    v_copy.wait_recv()
    xt[:, own:] = jnp.zeros((rank, xt.shape[1] - own), jnp.float32)
    xt[:, :own] = fold(dot(split(v_own + v_recv[...]), xf[mine], NT))
    m1, m2 = m // 2, m // 2 // chips

    @pl.when(mp == 0)
    def _():
        qf[:, :m1] = qf[:, :m1] + xt[...]

    @pl.when(mp == 1)
    def _():
        qf[:, features - m1 : features] = qf[:, features - m1 : features] + pltpu.roll(xt[...], m1 - own, 1)

    a1 = part(core * m1, m1)
    a2 = part(core * m1 + place * m2, m2)
    copy = send(qf.at[:, part((1 - core) * m1, m1)], q1, core_mate)
    start_x(STEPS[5])
    p_hat = exact(lower, mean)
    basis_ref[...] = p_hat * jnp.sqrt(jnp.float32(n * lax.axis_size("mp")))
    pair_ref[...] = split(p_hat)
    copy.wait_recv()
    q1[...] = exact(lower, (qf[:, a1] + q1[...]) * (1.0 / n_dp))
    qb[...] = q1[...].astype(jnp.bfloat16)
    copies = [
        send(qb.at[:, part(there * m2, m2)], q2.at[k], mate)
        for k, (there, mate) in enumerate(zip(places, peers))
    ]
    start_x(STEPS[6])
    merge_other(0, flat // 3)
    total = q1[:, part(place * m2, m2)]
    for k, copy in enumerate(copies):
        copy.wait_recv()
        total = total + q2[k].astype(jnp.float32)
    y1[...] = total.astype(jnp.bfloat16)
    copy = send(y1, y2, y_mate)
    start_x(STEPS[7])
    copy.wait_recv()
    qg_ref[:, a2] = (total + y2[...].astype(jnp.float32)).astype(jnp.bfloat16)
    copies = [send(qg_ref.at[:, a2], qg_ref.at[:, a2], mate) for mate in peers]
    start_x(pieces)
    merge_other(flat // 3, flat // 3 * 2)
    for copy in copies:
        copy.wait_recv()
    copy = send(qg_ref.at[:, a1], qg_ref.at[:, a1], core_mate)
    merge_other(flat // 3 * 2, flat)
    land_x(pieces)
    merge(flat, LANES)
    copy.wait_recv()
    for copy in sent + flying:
        copy.wait_send()


STEPS = (0, 2, 4, 4, 6, 1, 5, 1)


def residue_kernel(merged_ref, pair_ref, basis_ref, qg_ref, out_hbm, basis_out, own_out, tiles, sems):
    own = own_out.shape[1]
    features = merged_ref.shape[1]
    wide = tiles.shape[2]
    copies = []
    for step, lo in enumerate(range(0, features, wide)):
        hi = min(lo + wide, features)
        slot = step % tiles.shape[0]
        if step >= tiles.shape[0]:
            copies[step - tiles.shape[0]].wait()
        factor = qg_ref[:, lo:hi]
        approx = dot(pair_ref[...], jnp.concatenate([factor, factor], axis=0), TN)
        tiles[slot, :, : hi - lo] = (merged_ref[:, lo:hi] - approx).astype(jnp.bfloat16)
        copy = pltpu.make_async_copy(tiles.at[slot, :, : hi - lo], out_hbm.at[:, lo:hi], sems.at[slot])
        copy.start()
        copies.append(copy)
    basis_out[...] = basis_ref[...]
    mp = lax.axis_index("mp")

    @pl.when(mp == 0)
    def _():
        own_out[...] = qg_ref[:, :own].astype(jnp.float32)

    @pl.when(mp == 1)
    def _():
        begin = own // LANES * LANES
        late = qg_ref[:, begin:features].astype(jnp.float32)
        width = features - begin
        own_out[...] = pltpu.roll(late, own, 1)[:, :own]

    for copy in copies[-tiles.shape[0] :]:
        copy.wait()


def per_device(inputs, grad_out, error, q_prev):
    n_dp = lax.axis_size("dp")
    chips = n_dp // 2
    tokens, own = inputs.shape
    n, features = error.shape
    rank = q_prev.shape[1]
    m = -(-features // 1024) * 1024
    f32, bf16 = jnp.float32, jnp.bfloat16
    vmem, anywhere = pl.BlockSpec(memory_space=pltpu.VMEM), pl.BlockSpec(memory_space=pl.ANY)
    copies = 4 + 2 * chips + 5 + 2 * chips + 1
    merged, pair, basis, qg = pl.pallas_call(
        functools.partial(exchange_kernel, n_dp),
        out_shape=(
            pltpu.VMEM((n, features), f32),
            pltpu.VMEM((2 * rank, n), bf16),
            pltpu.VMEM((rank, n), f32),
            pltpu.VMEM((rank, m), bf16),
        ),
        in_specs=[pl.BlockSpec(memory_space=pltpu.HBM)] * 4,
        out_specs=(vmem,) * 4,
        scratch_shapes=[
            pltpu.VMEM((tokens, n), bf16),
            pltpu.VMEM((rank, own), f32),
            pltpu.VMEM((n, features), bf16),
            pltpu.VMEM((features, tokens), bf16),
            pltpu.VMEM((2, 2 * rank, own), bf16),
            pltpu.VMEM((rank, tokens), f32),
            pltpu.VMEM((rank, tokens), f32),
            pltpu.VMEM((rank, tokens), f32),
            pltpu.VMEM((rank, tokens), f32),
            pltpu.VMEM((rank, n), f32),
            pltpu.VMEM((rank, n // 2), f32),
            pltpu.VMEM((chips - 1, rank // chips, n // 2), f32),
            pltpu.VMEM((rank, n), f32),
            pltpu.VMEM((4, rank, rank), f32),
            pltpu.VMEM((rank, m), f32),
            pltpu.VMEM((rank, m // 2), f32),
            pltpu.VMEM((rank, m // 2), f32),
            pltpu.VMEM((rank, m // 2), bf16),
            pltpu.VMEM((chips - 1, rank, m // 2 // chips), bf16),
            pltpu.VMEM((rank, m // 2 // chips), bf16),
            pltpu.VMEM((rank, m // 2 // chips), bf16),
            pltpu.SemaphoreType.DMA((4,)),
            pltpu.SemaphoreType.DMA((own // PIECE,)),
            pltpu.SemaphoreType.DMA((own // PIECE,)),
            pltpu.SemaphoreType.DMA((copies,)),
            pltpu.SemaphoreType.DMA((copies,)),
        ],
        compiler_params=pltpu.CompilerParams(
            collective_id=0, has_side_effects=True, vmem_limit_bytes=36 * 1024 * 1024
        ),
        name="exchange",
    )(*(pltpu.with_memory_space_constraint(a, pltpu.HBM) for a in (inputs.T, grad_out, error, q_prev.T)))

    wide = m // 8
    new_error, basis, q_own = pl.pallas_call(
        residue_kernel,
        out_shape=(
            jax.ShapeDtypeStruct(error.shape, bf16),
            jax.ShapeDtypeStruct((rank, n), f32),
            jax.ShapeDtypeStruct((rank, own), f32),
        ),
        in_specs=[vmem] * 4,
        out_specs=(anywhere, vmem, vmem),
        scratch_shapes=[pltpu.VMEM((4, n, wide), bf16), pltpu.SemaphoreType.DMA((4,))],
        compiler_params=pltpu.CompilerParams(vmem_limit_bytes=16 * 1024 * 1024),
        name="residue",
    )(merged, pair, basis, qg)
    return new_error, basis.T, q_own.T


def general_form(inputs, grad_out, error, q_prev):
    highest = lax.Precision.HIGHEST
    replicas = lax.axis_size("dp")
    shards = lax.axis_size("mp")
    own_rows = grad_out.shape[1]
    rank = q_prev.shape[1]
    q_full = lax.all_gather(q_prev, "mp", axis=0, tiled=True)
    prod = lax.dot_general(
        grad_out,
        lax.all_gather(inputs, "mp", axis=1, tiled=True),
        (((0,), (0,)), ((), ())),
        preferred_element_type=jnp.float32,
    )
    merged = prod + error.astype(jnp.float32)
    local_p = jnp.dot(merged, q_full, precision=highest)
    factor = lax.psum(local_p, "dp") / replicas
    gram = lax.psum(jnp.dot(factor.T, factor, precision=highest), "mp")
    ridge = 0.01 * jnp.trace(gram) / rank + 1e-06
    gram = gram + ridge * jnp.eye(rank, dtype=jnp.float32)
    lower = jnp.linalg.cholesky(gram)
    p_hat = jax.scipy.linalg.solve_triangular(lower, factor.T, lower=True).T
    q_term = lax.dot_general(merged, p_hat, (((0,), (0,)), ((), ())), precision=highest)
    q_part = lax.psum_scatter(
        q_term.astype(jnp.bfloat16), "mp", scatter_dimension=0, tiled=True
    ).astype(jnp.float32)
    q_own = lax.psum(q_part, "dp") / replicas
    q_whole = lax.all_gather(q_own.astype(jnp.bfloat16), "mp", axis=0, tiled=True).astype(
        q_own.dtype
    )
    approx = jnp.dot(p_hat, q_whole.T, precision=highest)
    new_error = (merged - approx).astype(jnp.bfloat16)
    scale = jnp.sqrt(jnp.float32(own_rows * shards))
    return (new_error, p_hat * scale, q_own)


def solution(mesh):
    paired = mesh.shape["mp"] == 2 and mesh.shape["dp"] % 4 == 0 and mesh.shape["dp"] > 4
    return jax.shard_map(
        per_device if paired else general_form,
        mesh=mesh,
        in_specs=(P("dp", "mp"), P("dp", "mp"), P(("dp", "mp"), None), P("mp", None)),
        out_specs=(P(("dp", "mp"), None), P("mp", None), P("mp", None)),
        check_vma=False,
    )
```

```python
import functools

import jax
import jax.numpy as jnp
from jax import lax
from jax.experimental import pallas as pl
from jax.experimental.pallas import tpu as pltpu
from jax.sharding import PartitionSpec as P

MESH = pl.DeviceIdType.MESH
PIECE = 64
NN = (((1,), (0,)), ((), ()))
NT = (((1,), (1,)), ((), ()))
TN = (((0,), (0,)), ((), ()))
TT = (((0,), (1,)), ((), ()))
LANES = 128


def dot(a, b, dims=NN):
    return lax.dot_general(a, b, dims, preferred_element_type=jnp.float32)


def exact(a, b, dims=NN):
    return lax.dot_general(a, b, dims, precision=lax.Precision.HIGHEST, preferred_element_type=jnp.float32)


def split(value):
    head = value.astype(jnp.bfloat16)
    rest = (value - head.astype(jnp.float32)).astype(jnp.bfloat16)
    return jnp.concatenate([head, rest], axis=0)


def fold(terms):
    rank = terms.shape[0] // 2
    return terms[:rank] + terms[rank:]


def inverse_factor(gram):
    rank = gram.shape[0]
    row = lax.broadcasted_iota(jnp.int32, gram.shape, 0)
    diag = row == lax.broadcasted_iota(jnp.int32, gram.shape, 1)
    ridge = 0.01 * jnp.sum(jnp.where(diag, gram, 0.0), keepdims=True) / rank + 1e-06
    work = jnp.concatenate([gram + jnp.where(diag, ridge, 0.0), jnp.where(diag, 1.0, 0.0)], axis=1)
    wide = 2 * rank
    blocks = [work[i : i + 8] for i in range(0, rank, 8)]
    row8 = lax.broadcasted_iota(jnp.int32, (8, wide), 0)
    per = 8
    for k in range(0, rank, per):
        first = k // 8
        live = range(first, rank // 8)
        cols = [{i: jnp.broadcast_to(blocks[i][:, j : j + 1], (8, wide)) for i in live} for j in range(k, k + per)]
        at = k % 8
        rows = [blocks[first][at + j : at + j + 1] for j in range(per)]
        for s in range(0, per, 2):
            def pick(j, i):
                return cols[j][first][at + i : at + i + 1]
            a, b, c = pick(s, s), pick(s + 1, s), pick(s + 1, s + 1)
            ra, rdet = 1.0 / a, 1.0 / (a * c - b * b)
            ratio = b * ra
            follow = rows[s + 1] - ratio * rows[s]
            scale = a * rdet
            f0, f1 = {}, {}
            for i in live:
                x = cols[s][i] * ra
                if i == first:
                    x = jnp.where(row8 > at + s, x, 0.0)
                y = (cols[s + 1][i] - x * b) * scale
                if i == first:
                    y = jnp.where(row8 > at + s + 1, y, 0.0)
                f0[i], f1[i] = x, y
            for j in range(s + 2, per):
                top = pick(j, s)
                low = pick(j, s + 1) - ratio * top
                cols[j] = {i: cols[j][i] - f0[i] * top - f1[i] * low for i in live}
                here = slice(at + j, at + j + 1)
                rows[j] = rows[j] - f0[first][here] * rows[s] - f1[first][here] * follow
            for i in live:
                blocks[i] = blocks[i] - f0[i] * rows[s] - f1[i] * follow
    work = jnp.concatenate(blocks, axis=0)
    pivots = jnp.sum(jnp.where(diag, work[:, :rank], 0.0), axis=1, keepdims=True)
    return work[:, rank:] * lax.rsqrt(pivots)


def apply(factor, value):
    head = factor.astype(jnp.bfloat16)
    rest = (factor - head.astype(jnp.float32)).astype(jnp.bfloat16)
    pair = split(value)
    return dot(jnp.concatenate([head, head, rest], axis=1), jnp.concatenate([pair, pair[: value.shape[0]]], axis=0))


def exchange_kernel(
    n_dp, x_hbm, g_hbm, e_hbm, q_hbm,
    merged_ref, pair_ref, basis_ref, qg_ref,
    g_ref, q_ref, e_ref, xf, qs, u_send, u_recv, v_send, v_recv, pw, p1, p2, pg, gs, qf, xt, q1, qb, q2, y1, y2,
    load_sem, x_ssem, x_rsem, ssem, rsem,
):
    dp, mp = lax.axis_index("dp"), lax.axis_index("mp")
    core, xx, zz = lax.rem(dp, 2), lax.rem(dp // 2, 2), dp // 4
    n_z = n_dp // 4
    chips = n_dp // 2
    rank, own = q_ref.shape
    n, features = merged_ref.shape
    m = qf.shape[1]

    def device(d_core, d_x, d_y, k):
        z = lax.rem(zz + k, n_z)
        c = 1 - core if d_core else core
        x = 1 - xx if d_x else xx
        return ((z * 2 + x) * 2 + c, 1 - mp if d_y else mp)

    core_mate, y_mate, cross_mate = device(1, 0, 0, 0), device(0, 0, 1, 0), device(1, 0, 1, 0)
    offsets = [(a, k) for a in (1, 0) for k in range(n_z) if (a, k) != (0, 0)]
    peers = [device(0, a, 0, k) for a, k in offsets]
    places = [(1 - xx if a else xx) * n_z + lax.rem(zz + k, n_z) for a, k in offsets]
    origins = [(1 - xx if a else xx) * n_z + lax.rem(zz + n_z - k, n_z) for a, k in offsets]
    place = xx * n_z + zz
    near = 1 - 2 * lax.rem(zz, 2) + n_z
    squad = [device(0, 1, 0, 0), device(0, 0, 0, near), device(0, 1, 0, near)]

    x_base = pl.multiple_of(mp * own, PIECE)
    mine = pl.ds(x_base, own)
    load_x = pltpu.make_async_copy(x_hbm, xf.at[mine], load_sem.at[0])
    load_e = pltpu.make_async_copy(e_hbm, e_ref, load_sem.at[1])
    load_g = pltpu.make_async_copy(g_hbm, g_ref, load_sem.at[2])
    load_q = pltpu.make_async_copy(q_hbm, q_ref, load_sem.at[3])
    load_q.start()
    load_x.start()
    load_g.start()
    load_e.start()
    barrier = pltpu.get_barrier_semaphore()
    mates = [core_mate, y_mate, cross_mate] + peers
    for mate in mates:
        pl.semaphore_signal(barrier, inc=1, device_id=mate, device_id_type=MESH)

    sent = []

    def send(src, dst, mate):
        index = len(sent)
        copy = pltpu.make_async_remote_copy(
            src_ref=src, dst_ref=dst, send_sem=ssem.at[index], recv_sem=rsem.at[index],
            device_id=mate, device_id_type=MESH,
        )
        copy.start()
        sent.append(copy)
        return copy

    pieces = own // PIECE
    flat = own // LANES * LANES
    middle = pl.multiple_of(mp * own + (1 - mp) * flat, PIECE)
    flying = []

    def start_x(count):
        for j in range(len(flying), min(pieces, len(flying) + count)):
            row = middle if j == pieces - 1 else x_base + mp * PIECE + j * PIECE
            part = pl.ds(pl.multiple_of(row, PIECE), PIECE)
            copy = pltpu.make_async_remote_copy(
                src_ref=xf.at[part], dst_ref=xf.at[part], send_sem=x_ssem.at[j], recv_sem=x_rsem.at[j],
                device_id=y_mate, device_id_type=MESH,
            )
            copy.start()
            flying.append(copy)

    landed = [0]

    def land_x(count):
        for copy in flying[landed[0] : count]:
            copy.wait_recv()
        landed[0] = max(landed[0], count)

    def merge(begin, size):
        columns = pl.ds(pl.multiple_of(begin, LANES), size)
        product = dot(g_ref[...], xf[columns, :], TT)
        merged_ref[:, columns] = product + e_ref[:, columns].astype(jnp.float32)

    def merge_own(step):
        size = flat // 3
        merge(mp * (flat + LANES) + step * size, size)

    def merge_other(begin, end):
        land_x(end // PIECE)
        merge((1 - mp) * (flat + LANES) + begin, end - begin)

    load_q.wait()
    q_own = q_ref[...]
    edge = qs.shape[2] - own
    shifted = pltpu.roll(jnp.concatenate([q_own, jnp.zeros((rank, edge), jnp.float32)], axis=1), mp * edge, 1)
    qs[mp] = split(shifted)
    pl.semaphore_wait(barrier, len(mates))
    piece = 2 * rank // 8
    corner = xx * 2 + lax.rem(zz, 2)

    def q_rows(where):
        return pl.ds(pl.multiple_of(core * rank + where * piece, piece), piece)

    q_copy = send(qs.at[mp, q_rows(corner)], qs.at[mp, q_rows(corner)], y_mate)
    load_x.wait()
    u_own = fold(dot(split(q_own), xf[mine]))
    u_send[...] = u_own
    u_copy = send(u_send, u_recv, y_mate)
    start_x(STEPS[0])
    load_g.wait()
    load_e.wait()

    def e_q(half):
        columns = pl.ds(pl.multiple_of(half * (features - qs.shape[2]), LANES), qs.shape[2])
        return fold(dot(qs[half], e_ref[:, columns], NT))

    pw[...] = e_q(mp)
    q_copy.wait_recv()
    theirs = 1 - mp
    copies = [send(qs.at[theirs, q_rows(corner)], qs.at[theirs, q_rows(corner)], mate) for mate in squad]
    q_pass = [send(qs.at[theirs, q_rows(corner)], qs.at[theirs, q_rows(corner)], core_mate)]
    start_x(STEPS[8])
    merge_own(0)
    corners = [corner + 2 - 4 * xx, corner + 1 - 2 * lax.rem(zz, 2), 3 - corner]
    for copy, where in zip(copies, corners):
        copy.wait_recv()
        q_pass.append(send(qs.at[theirs, q_rows(where)], qs.at[theirs, q_rows(where)], core_mate))
    u_copy.wait_recv()
    pw[...] = pw[...] + fold(dot(split(u_own + u_recv[...]), g_ref[...]))
    for copy in q_pass:
        copy.wait_recv()
    pw[...] = pw[...] + e_q(theirs)

    def part(offset, size):
        return pl.ds(pl.multiple_of(offset, size), size)

    n1, height = n // 2, rank // chips
    b1 = part(core * n1, n1)
    level = part(place * height, height)
    copy = send(pw.at[:, part((1 - core) * n1, n1)], p1, core_mate)
    start_x(STEPS[1])
    copy.wait_recv()
    pw[:, b1] = pw[:, b1] + p1[...]
    copies = [
        send(pw.at[part(there * height, height), b1], p2.at[k], mate)
        for k, (there, mate) in enumerate(zip(places, peers))
    ]
    start_x(STEPS[2])
    merge_own(1)
    total = pw[level, b1]
    for k, copy in enumerate(copies):
        copy.wait_recv()
        total = total + p2[k]
    pg[level, b1] = total * (1.0 / n_dp)
    copies = [send(pg.at[level, b1], pg.at[level, b1], mate) for mate in peers]
    p_pass = [send(pg.at[level, b1], pg.at[level, b1], core_mate)]
    start_x(STEPS[3])
    merge_own(2)
    for copy, there in zip(copies, origins):
        copy.wait_recv()
        block = part(there * height, height)
        p_pass.append(send(pg.at[block, b1], pg.at[block, b1], core_mate))

    p_half = pg[:, b1]
    slot = mp * 2 + core
    gs[slot] = exact(p_half, p_half, NT)
    grams = [send(gs.at[slot], gs.at[slot], mate) for mate in (y_mate, cross_mate, core_mate)]
    for copy in p_pass:
        copy.wait_recv()
    mean = pg[...]
    mean_pair = split(mean)
    v_own = fold(dot(mean_pair, g_ref[...], NT))
    v_send[...] = v_own
    v_copy = send(v_send, v_recv, y_mate)
    start_x(STEPS[4])
    qf[:, features:] = jnp.zeros((rank, m - features), jnp.float32)
    for lo in range(0, features, m // 4):
        hi = min(lo + m // 4, features)
        qf[:, lo:hi] = fold(dot(mean_pair, e_ref[:, lo:hi]))
    for copy in grams:
        copy.wait_recv()
    lower = inverse_factor(gs[0] + gs[1] + gs[2] + gs[3])

    v_copy.wait_recv()
    xt[:, own:] = jnp.zeros((rank, xt.shape[1] - own), jnp.float32)
    xt[:, :own] = fold(dot(split(v_own + v_recv[...]), xf[mine], NT))
    m1, m2 = m // 2, m // 2 // chips

    @pl.when(mp == 0)
    def _():
        qf[:, :m1] = qf[:, :m1] + xt[...]

    @pl.when(mp == 1)
    def _():
        qf[:, features - m1 : features] = qf[:, features - m1 : features] + pltpu.roll(xt[...], m1 - own, 1)

    a2 = part(core * m1 + place * m2, m2)
    m3 = m1 // 2
    groups = (1 - xx, xx)
    halves = [send(qf.at[:, part((1 - core) * m1 + there * m3, m3)], q1.at[:, part(there * m3, m3)], core_mate) for there in groups]
    start_x(STEPS[5])
    p_hat = exact(lower, mean)
    basis_ref[...] = p_hat * jnp.sqrt(jnp.float32(n * lax.axis_size("mp")))
    pair_ref[...] = split(p_hat)
    copies = []
    for copy, there in zip(halves, groups):
        copy.wait_recv()
        columns = part(there * m3, m3)
        value = apply(lower, (qf[:, part(core * m1 + there * m3, m3)] + q1[:, columns]) * (1.0 / n_dp))
        q1[:, columns] = value
        qb[:, columns] = value.astype(jnp.bfloat16)
        for k in range(len(copies), n_z if there is groups[0] else chips - 1):
            copies.append(send(qb.at[:, part(places[k] * m2, m2)], q2.at[k], peers[k]))
    start_x(STEPS[6])
    merge_other(0, flat // 3)
    total = q1[:, part(place * m2, m2)]
    for k, copy in enumerate(copies):
        copy.wait_recv()
        total = total + q2[k].astype(jnp.float32)
    y1[...] = total.astype(jnp.bfloat16)
    copy = send(y1, y2, y_mate)
    start_x(STEPS[7])
    copy.wait_recv()
    qg_ref[:, a2] = (total + y2[...].astype(jnp.float32)).astype(jnp.bfloat16)
    copies = [send(qg_ref.at[:, a2], qg_ref.at[:, a2], mate) for mate in peers]
    q_pass = [send(qg_ref.at[:, a2], qg_ref.at[:, a2], core_mate)]
    start_x(pieces)
    merge_other(flat // 3, flat // 3 * 2)
    for copy, there in zip(copies, origins):
        copy.wait_recv()
        columns = part(core * m1 + there * m2, m2)
        q_pass.append(send(qg_ref.at[:, columns], qg_ref.at[:, columns], core_mate))
    merge_other(flat // 3 * 2, flat // 15 * 13)
    merge_other(flat // 15 * 13, flat)
    land_x(pieces)
    merge(flat, LANES)
    for copy in q_pass:
        copy.wait_recv()
    for copy in sent + flying:
        copy.wait_send()


STEPS = (2, 2, 3, 3, 3, 1, 5, 2, 3)


def residue_kernel(merged_ref, pair_ref, basis_ref, qg_ref, out_hbm, basis_out, own_out, tiles, sems):
    own = own_out.shape[1]
    features = merged_ref.shape[1]
    wide = tiles.shape[2]
    copies = []
    for step, lo in enumerate(range(0, features, wide)):
        hi = min(lo + wide, features)
        slot = step % tiles.shape[0]
        if step >= tiles.shape[0]:
            copies[step - tiles.shape[0]].wait()
        factor = qg_ref[:, lo:hi]
        approx = dot(pair_ref[...], jnp.concatenate([factor, factor], axis=0), TN)
        tiles[slot, :, : hi - lo] = (merged_ref[:, lo:hi] - approx).astype(jnp.bfloat16)
        copy = pltpu.make_async_copy(tiles.at[slot, :, : hi - lo], out_hbm.at[:, lo:hi], sems.at[slot])
        copy.start()
        copies.append(copy)
    basis_out[...] = basis_ref[...]
    mp = lax.axis_index("mp")

    @pl.when(mp == 0)
    def _():
        own_out[...] = qg_ref[:, :own].astype(jnp.float32)

    @pl.when(mp == 1)
    def _():
        begin = own // LANES * LANES
        late = qg_ref[:, begin:features].astype(jnp.float32)
        width = features - begin
        own_out[...] = pltpu.roll(late, own, 1)[:, :own]

    for copy in copies[-tiles.shape[0] :]:
        copy.wait()


def per_device(inputs, grad_out, error, q_prev):
    n_dp = lax.axis_size("dp")
    chips = n_dp // 2
    tokens, own = inputs.shape
    n, features = error.shape
    rank = q_prev.shape[1]
    m = -(-features // 1024) * 1024
    f32, bf16 = jnp.float32, jnp.bfloat16
    vmem, anywhere = pl.BlockSpec(memory_space=pltpu.VMEM), pl.BlockSpec(memory_space=pl.ANY)
    copies = 10 + 3 * chips + 4 + 2 + 3 * chips
    merged, pair, basis, qg = pl.pallas_call(
        functools.partial(exchange_kernel, n_dp),
        out_shape=(
            pltpu.VMEM((n, features), f32),
            pltpu.VMEM((2 * rank, n), bf16),
            pltpu.VMEM((rank, n), f32),
            pltpu.VMEM((rank, m), bf16),
        ),
        in_specs=[pl.BlockSpec(memory_space=pltpu.HBM)] * 4,
        out_specs=(vmem,) * 4,
        scratch_shapes=[
            pltpu.VMEM((tokens, n), bf16),
            pltpu.VMEM((rank, own), f32),
            pltpu.VMEM((n, features), bf16),
            pltpu.VMEM((features, tokens), bf16),
            pltpu.VMEM((2, 2 * rank, -(-own // LANES) * LANES), bf16),
            pltpu.VMEM((rank, tokens), f32),
            pltpu.VMEM((rank, tokens), f32),
            pltpu.VMEM((rank, tokens), f32),
            pltpu.VMEM((rank, tokens), f32),
            pltpu.VMEM((rank, n), f32),
            pltpu.VMEM((rank, n // 2), f32),
            pltpu.VMEM((chips - 1, rank // chips, n // 2), f32),
            pltpu.VMEM((rank, n), f32),
            pltpu.VMEM((4, rank, rank), f32),
            pltpu.VMEM((rank, m), f32),
            pltpu.VMEM((rank, m // 2), f32),
            pltpu.VMEM((rank, m // 2), f32),
            pltpu.VMEM((rank, m // 2), bf16),
            pltpu.VMEM((chips - 1, rank, m // 2 // chips), bf16),
            pltpu.VMEM((rank, m // 2 // chips), bf16),
            pltpu.VMEM((rank, m // 2 // chips), bf16),
            pltpu.SemaphoreType.DMA((4,)),
            pltpu.SemaphoreType.DMA((own // PIECE,)),
            pltpu.SemaphoreType.DMA((own // PIECE,)),
            pltpu.SemaphoreType.DMA((copies,)),
            pltpu.SemaphoreType.DMA((copies,)),
        ],
        compiler_params=pltpu.CompilerParams(
            collective_id=0, has_side_effects=True, vmem_limit_bytes=36 * 1024 * 1024
        ),
        name="exchange",
    )(*(pltpu.with_memory_space_constraint(a, pltpu.HBM) for a in (inputs.T, grad_out, error, q_prev.T)))

    wide = m // 8
    new_error, basis, q_own = pl.pallas_call(
        residue_kernel,
        out_shape=(
            jax.ShapeDtypeStruct(error.shape, bf16),
            jax.ShapeDtypeStruct((rank, n), f32),
            jax.ShapeDtypeStruct((rank, own), f32),
        ),
        in_specs=[vmem] * 4,
        out_specs=(anywhere, vmem, vmem),
        scratch_shapes=[pltpu.VMEM((4, n, wide), bf16), pltpu.SemaphoreType.DMA((4,))],
        compiler_params=pltpu.CompilerParams(vmem_limit_bytes=16 * 1024 * 1024),
        name="residue",
    )(merged, pair, basis, qg)
    return new_error, basis.T, q_own.T


def general_form(inputs, grad_out, error, q_prev):
    highest = lax.Precision.HIGHEST
    replicas = lax.axis_size("dp")
    shards = lax.axis_size("mp")
    own_rows = grad_out.shape[1]
    rank = q_prev.shape[1]
    q_full = lax.all_gather(q_prev, "mp", axis=0, tiled=True)
    prod = lax.dot_general(
        grad_out,
        lax.all_gather(inputs, "mp", axis=1, tiled=True),
        (((0,), (0,)), ((), ())),
        preferred_element_type=jnp.float32,
    )
    merged = prod + error.astype(jnp.float32)
    local_p = jnp.dot(merged, q_full, precision=highest)
    factor = lax.psum(local_p, "dp") / replicas
    gram = lax.psum(jnp.dot(factor.T, factor, precision=highest), "mp")
    ridge = 0.01 * jnp.trace(gram) / rank + 1e-06
    gram = gram + ridge * jnp.eye(rank, dtype=jnp.float32)
    lower = jnp.linalg.cholesky(gram)
    p_hat = jax.scipy.linalg.solve_triangular(lower, factor.T, lower=True).T
    q_term = lax.dot_general(merged, p_hat, (((0,), (0,)), ((), ())), precision=highest)
    q_part = lax.psum_scatter(
        q_term.astype(jnp.bfloat16), "mp", scatter_dimension=0, tiled=True
    ).astype(jnp.float32)
    q_own = lax.psum(q_part, "dp") / replicas
    q_whole = lax.all_gather(q_own.astype(jnp.bfloat16), "mp", axis=0, tiled=True).astype(
        q_own.dtype
    )
    approx = jnp.dot(p_hat, q_whole.T, precision=highest)
    new_error = (merged - approx).astype(jnp.bfloat16)
    scale = jnp.sqrt(jnp.float32(own_rows * shards))
    return (new_error, p_hat * scale, q_own)


def solution(mesh):
    paired = mesh.shape["mp"] == 2 and mesh.shape["dp"] % 4 == 0 and mesh.shape["dp"] > 4
    return jax.shard_map(
        per_device if paired else general_form,
        mesh=mesh,
        in_specs=(P("dp", "mp"), P("dp", "mp"), P(("dp", "mp"), None), P("mp", None)),
        out_specs=(P(("dp", "mp"), None), P("mp", None), P("mp", None)),
        check_vma=False,
    )
```

```python
import functools

import jax
import jax.numpy as jnp
from jax import lax
from jax.experimental import pallas as pl
from jax.experimental.pallas import tpu as pltpu
from jax.sharding import PartitionSpec as P

MESH = pl.DeviceIdType.MESH
PIECE = 64
NN = (((1,), (0,)), ((), ()))
NT = (((1,), (1,)), ((), ()))
TN = (((0,), (0,)), ((), ()))
TT = (((0,), (1,)), ((), ()))
LANES = 128


def dot(a, b, dims=NN):
    return lax.dot_general(a, b, dims, preferred_element_type=jnp.float32)


def exact(a, b, dims=NN):
    return lax.dot_general(a, b, dims, precision=lax.Precision.HIGHEST, preferred_element_type=jnp.float32)


def split(value):
    head = value.astype(jnp.bfloat16)
    rest = (value - head.astype(jnp.float32)).astype(jnp.bfloat16)
    return jnp.concatenate([head, rest], axis=0)


def fold(terms):
    rank = terms.shape[0] // 2
    return terms[:rank] + terms[rank:]


def inverse_factor(gram):
    rank = gram.shape[0]
    row = lax.broadcasted_iota(jnp.int32, gram.shape, 0)
    diag = row == lax.broadcasted_iota(jnp.int32, gram.shape, 1)
    ridge = 0.01 * jnp.sum(jnp.where(diag, gram, 0.0), keepdims=True) / rank + 1e-06
    work = jnp.concatenate([gram + jnp.where(diag, ridge, 0.0), jnp.where(diag, 1.0, 0.0)], axis=1)
    wide = 2 * rank
    blocks = [work[i : i + 8] for i in range(0, rank, 8)]
    row8 = lax.broadcasted_iota(jnp.int32, (8, wide), 0)
    per = 8
    for k in range(0, rank, per):
        first = k // 8
        live = range(first, rank // 8)
        cols = [{i: jnp.broadcast_to(blocks[i][:, j : j + 1], (8, wide)) for i in live} for j in range(k, k + per)]
        at = k % 8
        rows = [blocks[first][at + j : at + j + 1] for j in range(per)]
        for s in range(0, per, 2):
            def pick(j, i):
                return cols[j][first][at + i : at + i + 1]
            a, b, c = pick(s, s), pick(s + 1, s), pick(s + 1, s + 1)
            ra, rdet = 1.0 / a, 1.0 / (a * c - b * b)
            ratio = b * ra
            follow = rows[s + 1] - ratio * rows[s]
            scale = a * rdet
            f0, f1 = {}, {}
            for i in live:
                x = cols[s][i] * ra
                if i == first:
                    x = jnp.where(row8 > at + s, x, 0.0)
                y = (cols[s + 1][i] - x * b) * scale
                if i == first:
                    y = jnp.where(row8 > at + s + 1, y, 0.0)
                f0[i], f1[i] = x, y
            for j in range(s + 2, per):
                top = pick(j, s)
                low = pick(j, s + 1) - ratio * top
                cols[j] = {i: cols[j][i] - f0[i] * top - f1[i] * low for i in live}
                here = slice(at + j, at + j + 1)
                rows[j] = rows[j] - f0[first][here] * rows[s] - f1[first][here] * follow
            for i in live:
                blocks[i] = blocks[i] - f0[i] * rows[s] - f1[i] * follow
    work = jnp.concatenate(blocks, axis=0)
    pivots = jnp.sum(jnp.where(diag, work[:, :rank], 0.0), axis=1, keepdims=True)
    return work[:, rank:] * lax.rsqrt(pivots)


def apply(factor, value):
    head = factor.astype(jnp.bfloat16)
    rest = (factor - head.astype(jnp.float32)).astype(jnp.bfloat16)
    pair = split(value)
    return dot(jnp.concatenate([head, head, rest], axis=1), jnp.concatenate([pair, pair[: value.shape[0]]], axis=0))


def exchange_kernel(
    n_dp, x_hbm, g_hbm, e_hbm, q_hbm,
    out_ref, basis_ref, qown_ref,
    merged_ref, pair_ref, qg_ref, g_ref, q_ref, e_ref, xf, qs, u_send, u_recv, v_send, v_recv, pw, p1, p2, pg, gs, qf, xt, q1, qb, q2, y1, y2,
    load_sem, x_ssem, x_rsem, ssem, rsem,
):
    dp, mp = lax.axis_index("dp"), lax.axis_index("mp")
    core, xx, zz = lax.rem(dp, 2), lax.rem(dp // 2, 2), dp // 4
    n_z = n_dp // 4
    chips = n_dp // 2
    rank, own = q_ref.shape
    n, features = merged_ref.shape
    m = qf.shape[1]

    def device(d_core, d_x, d_y, k):
        z = lax.rem(zz + k, n_z)
        c = 1 - core if d_core else core
        x = 1 - xx if d_x else xx
        return ((z * 2 + x) * 2 + c, 1 - mp if d_y else mp)

    core_mate, y_mate, cross_mate = device(1, 0, 0, 0), device(0, 0, 1, 0), device(1, 0, 1, 0)
    offsets = [(a, k) for a in (1, 0) for k in range(n_z) if (a, k) != (0, 0)]
    peers = [device(0, a, 0, k) for a, k in offsets]
    places = [(1 - xx if a else xx) * n_z + lax.rem(zz + k, n_z) for a, k in offsets]
    origins = [(1 - xx if a else xx) * n_z + lax.rem(zz + n_z - k, n_z) for a, k in offsets]
    place = xx * n_z + zz
    near = 1 - 2 * lax.rem(zz, 2) + n_z
    squad = [device(0, 1, 0, 0), device(0, 0, 0, near), device(0, 1, 0, near)]

    x_base = pl.multiple_of(mp * own, PIECE)
    mine = pl.ds(x_base, own)
    load_x = pltpu.make_async_copy(x_hbm, xf.at[mine], load_sem.at[0])
    load_e = pltpu.make_async_copy(e_hbm, e_ref, load_sem.at[1])
    load_g = pltpu.make_async_copy(g_hbm, g_ref, load_sem.at[2])
    load_q = pltpu.make_async_copy(q_hbm, q_ref, load_sem.at[3])
    load_q.start()
    load_x.start()
    load_g.start()
    load_e.start()
    barrier = pltpu.get_barrier_semaphore()
    mates = [core_mate, y_mate, cross_mate] + peers
    for mate in mates:
        pl.semaphore_signal(barrier, inc=1, device_id=mate, device_id_type=MESH)

    sent = []

    def send(src, dst, mate):
        index = len(sent)
        copy = pltpu.make_async_remote_copy(
            src_ref=src, dst_ref=dst, send_sem=ssem.at[index], recv_sem=rsem.at[index],
            device_id=mate, device_id_type=MESH,
        )
        copy.start()
        sent.append(copy)
        return copy

    pieces = own // PIECE
    flat = own // LANES * LANES
    middle = pl.multiple_of(mp * own + (1 - mp) * flat, PIECE)
    flying = []

    def start_x(count):
        for j in range(len(flying), min(pieces, len(flying) + count)):
            row = middle if j == pieces - 1 else x_base + mp * PIECE + j * PIECE
            part = pl.ds(pl.multiple_of(row, PIECE), PIECE)
            copy = pltpu.make_async_remote_copy(
                src_ref=xf.at[part], dst_ref=xf.at[part], send_sem=x_ssem.at[j], recv_sem=x_rsem.at[j],
                device_id=y_mate, device_id_type=MESH,
            )
            copy.start()
            flying.append(copy)

    landed = [0]

    def land_x(count):
        for copy in flying[landed[0] : count]:
            copy.wait_recv()
        landed[0] = max(landed[0], count)

    def merge(begin, size):
        columns = pl.ds(pl.multiple_of(begin, LANES), size)
        product = dot(g_ref[...], xf[columns, :], TT)
        merged_ref[:, columns] = product + e_ref[:, columns].astype(jnp.float32)

    def merge_own(step):
        size = flat // 3
        merge(mp * (flat + LANES) + step * size, size)

    def merge_other(begin, end):
        land_x(end // PIECE)
        merge((1 - mp) * (flat + LANES) + begin, end - begin)

    load_q.wait()
    q_own = q_ref[...]
    edge = qs.shape[2] - own
    shifted = pltpu.roll(jnp.concatenate([q_own, jnp.zeros((rank, edge), jnp.float32)], axis=1), mp * edge, 1)
    qs[mp] = split(shifted)
    pl.semaphore_wait(barrier, len(mates))
    piece = 2 * rank // 8
    corner = xx * 2 + lax.rem(zz, 2)

    def q_rows(where):
        return pl.ds(pl.multiple_of(core * rank + where * piece, piece), piece)

    q_copy = send(qs.at[mp, q_rows(corner)], qs.at[mp, q_rows(corner)], y_mate)
    load_x.wait()
    u_own = fold(dot(split(q_own), xf[mine]))
    u_send[...] = u_own
    u_copy = send(u_send, u_recv, y_mate)
    start_x(STEPS[0])
    load_g.wait()
    load_e.wait()

    def e_q(half):
        columns = pl.ds(pl.multiple_of(half * (features - qs.shape[2]), LANES), qs.shape[2])
        return fold(dot(qs[half], e_ref[:, columns], NT))

    pw[...] = e_q(mp)
    q_copy.wait_recv()
    theirs = 1 - mp
    copies = [send(qs.at[theirs, q_rows(corner)], qs.at[theirs, q_rows(corner)], mate) for mate in squad]
    q_pass = [send(qs.at[theirs, q_rows(corner)], qs.at[theirs, q_rows(corner)], core_mate)]
    start_x(STEPS[8])
    merge_own(0)
    corners = [corner + 2 - 4 * xx, corner + 1 - 2 * lax.rem(zz, 2), 3 - corner]
    for copy, where in zip(copies, corners):
        copy.wait_recv()
        q_pass.append(send(qs.at[theirs, q_rows(where)], qs.at[theirs, q_rows(where)], core_mate))
    u_copy.wait_recv()
    pw[...] = pw[...] + fold(dot(split(u_own + u_recv[...]), g_ref[...]))
    for copy in q_pass:
        copy.wait_recv()
    pw[...] = pw[...] + e_q(theirs)

    def part(offset, size):
        return pl.ds(pl.multiple_of(offset, size), size)

    n1, height = n // 2, rank // chips
    b1 = part(core * n1, n1)
    level = part(place * height, height)
    copy = send(pw.at[:, part((1 - core) * n1, n1)], p1, core_mate)
    start_x(STEPS[1])
    copy.wait_recv()
    pw[:, b1] = pw[:, b1] + p1[...]
    copies = [
        send(pw.at[part(there * height, height), b1], p2.at[k], mate)
        for k, (there, mate) in enumerate(zip(places, peers))
    ]
    start_x(STEPS[2])
    merge_own(1)
    total = pw[level, b1]
    for k, copy in enumerate(copies):
        copy.wait_recv()
        total = total + p2[k]
    pg[level, b1] = total * (1.0 / n_dp)
    copies = [send(pg.at[level, b1], pg.at[level, b1], mate) for mate in peers]
    p_pass = [send(pg.at[level, b1], pg.at[level, b1], core_mate)]
    start_x(STEPS[3])
    merge_own(2)
    for copy, there in zip(copies, origins):
        copy.wait_recv()
        block = part(there * height, height)
        p_pass.append(send(pg.at[block, b1], pg.at[block, b1], core_mate))

    p_half = pg[:, b1]
    slot = mp * 2 + core
    gs[slot] = exact(p_half, p_half, NT)
    grams = [send(gs.at[slot], gs.at[slot], mate) for mate in (y_mate, cross_mate, core_mate)]
    for copy in p_pass:
        copy.wait_recv()
    mean = pg[...]
    mean_pair = split(mean)
    v_own = fold(dot(mean_pair, g_ref[...], NT))
    v_send[...] = v_own
    v_copy = send(v_send, v_recv, y_mate)
    start_x(STEPS[4])
    qf[:, features:] = jnp.zeros((rank, m - features), jnp.float32)
    for lo in range(0, features, m // 4):
        hi = min(lo + m // 4, features)
        qf[:, lo:hi] = fold(dot(mean_pair, e_ref[:, lo:hi]))
    for copy in grams:
        copy.wait_recv()
    lower = inverse_factor(gs[0] + gs[1] + gs[2] + gs[3])

    v_copy.wait_recv()
    xt[:, own:] = jnp.zeros((rank, xt.shape[1] - own), jnp.float32)
    xt[:, :own] = fold(dot(split(v_own + v_recv[...]), xf[mine], NT))
    m1, m2 = m // 2, m // 2 // chips

    @pl.when(mp == 0)
    def _():
        qf[:, :m1] = qf[:, :m1] + xt[...]

    @pl.when(mp == 1)
    def _():
        qf[:, features - m1 : features] = qf[:, features - m1 : features] + pltpu.roll(xt[...], m1 - own, 1)

    a2 = part(core * m1 + place * m2, m2)
    m3 = m1 // 2
    groups = (1 - xx, xx)
    halves = [send(qf.at[:, part((1 - core) * m1 + there * m3, m3)], q1.at[:, part(there * m3, m3)], core_mate) for there in groups]
    start_x(STEPS[5])
    p_hat = exact(lower, mean)
    basis_ref[...] = p_hat * jnp.sqrt(jnp.float32(n * lax.axis_size("mp")))
    pair_ref[...] = split(p_hat)
    copies = []
    for copy, there in zip(halves, groups):
        copy.wait_recv()
        columns = part(there * m3, m3)
        value = apply(lower, (qf[:, part(core * m1 + there * m3, m3)] + q1[:, columns]) * (1.0 / n_dp))
        q1[:, columns] = value
        qb[:, columns] = value.astype(jnp.bfloat16)
        for k in range(len(copies), n_z if there is groups[0] else chips - 1):
            copies.append(send(qb.at[:, part(places[k] * m2, m2)], q2.at[k], peers[k]))
    start_x(STEPS[6])
    merge_other(0, flat // 3)
    total = q1[:, part(place * m2, m2)]
    for k, copy in enumerate(copies):
        copy.wait_recv()
        total = total + q2[k].astype(jnp.float32)
    y1[...] = total.astype(jnp.bfloat16)
    copy = send(y1, y2, y_mate)
    start_x(STEPS[7])
    copy.wait_recv()
    qg_ref[:, a2] = (total + y2[...].astype(jnp.float32)).astype(jnp.bfloat16)
    copies = [send(qg_ref.at[:, a2], qg_ref.at[:, a2], mate) for mate in peers]
    q_pass = [send(qg_ref.at[:, a2], qg_ref.at[:, a2], core_mate)]
    start_x(pieces)
    merge_other(flat // 3, flat // 3 * 2)
    for copy, there in zip(copies, origins):
        copy.wait_recv()
        columns = part(core * m1 + there * m2, m2)
        q_pass.append(send(qg_ref.at[:, columns], qg_ref.at[:, columns], core_mate))
    for copy in q_pass:
        copy.wait_recv()

    def finish(begin, size):
        columns = pl.ds(pl.multiple_of(begin, LANES), size)
        factor = qg_ref[:, columns]
        approx = dot(pair_ref[...], jnp.concatenate([factor, factor], axis=0), TN)
        out_ref[:, columns] = (merged_ref[:, columns] - approx).astype(jnp.bfloat16)

    third, far = flat // 3, flat + LANES
    for step in range(3):
        finish(mp * far + step * third, third)
    for step in range(2):
        finish((1 - mp) * far + step * third, third)

    @pl.when(mp == 0)
    def _():
        qown_ref[...] = qg_ref[:, :own].astype(jnp.float32)

    @pl.when(mp == 1)
    def _():
        late = qg_ref[:, flat:features].astype(jnp.float32)
        qown_ref[...] = pltpu.roll(late, own, 1)[:, :own]

    for begin, end in ((2 * third, 2 * third + 3 * LANES), (2 * third + 3 * LANES, flat)):
        merge_other(begin, end)
        finish((1 - mp) * far + begin, end - begin)
    land_x(pieces)
    merge(flat, LANES)
    finish(flat, LANES)
    for copy in sent + flying:
        copy.wait_send()


STEPS = (2, 2, 3, 3, 3, 1, 5, 2, 3)


def store_kernel(*refs):
    sources, targets, sems = refs[:3], refs[3:6], refs[6]
    blocks = sems.shape[0] - 2
    size = sources[0].shape[0] // blocks
    copies = []
    for k in range(blocks):
        rows = pl.ds(k * size, size)
        copies.append(pltpu.make_async_copy(sources[0].at[rows], targets[0].at[rows], sems.at[k]))
    for k in (1, 2):
        copies.append(pltpu.make_async_copy(sources[k], targets[k], sems.at[blocks + k - 1]))
    for copy in copies:
        copy.start()
    for copy in copies:
        copy.wait()


def per_device(inputs, grad_out, error, q_prev):
    n_dp = lax.axis_size("dp")
    chips = n_dp // 2
    tokens, own = inputs.shape
    n, features = error.shape
    rank = q_prev.shape[1]
    m = -(-features // 1024) * 1024
    f32, bf16 = jnp.float32, jnp.bfloat16
    vmem, anywhere = pl.BlockSpec(memory_space=pltpu.VMEM), pl.BlockSpec(memory_space=pl.ANY)
    copies = 10 + 3 * chips + 4 + 2 + 3 * chips
    results = pl.pallas_call(
        functools.partial(exchange_kernel, n_dp),
        out_shape=(
            pltpu.VMEM((n, features), bf16),
            pltpu.VMEM((rank, n), f32),
            pltpu.VMEM((rank, own), f32),
        ),
        in_specs=[pl.BlockSpec(memory_space=pltpu.HBM)] * 4,
        out_specs=(vmem,) * 3,
        scratch_shapes=[
            pltpu.VMEM((n, features), f32),
            pltpu.VMEM((2 * rank, n), bf16),
            pltpu.VMEM((rank, m), bf16),
            pltpu.VMEM((tokens, n), bf16),
            pltpu.VMEM((rank, own), f32),
            pltpu.VMEM((n, features), bf16),
            pltpu.VMEM((features, tokens), bf16),
            pltpu.VMEM((2, 2 * rank, -(-own // LANES) * LANES), bf16),
            pltpu.VMEM((rank, tokens), f32),
            pltpu.VMEM((rank, tokens), f32),
            pltpu.VMEM((rank, tokens), f32),
            pltpu.VMEM((rank, tokens), f32),
            pltpu.VMEM((rank, n), f32),
            pltpu.VMEM((rank, n // 2), f32),
            pltpu.VMEM((chips - 1, rank // chips, n // 2), f32),
            pltpu.VMEM((rank, n), f32),
            pltpu.VMEM((4, rank, rank), f32),
            pltpu.VMEM((rank, m), f32),
            pltpu.VMEM((rank, m // 2), f32),
            pltpu.VMEM((rank, m // 2), f32),
            pltpu.VMEM((rank, m // 2), bf16),
            pltpu.VMEM((chips - 1, rank, m // 2 // chips), bf16),
            pltpu.VMEM((rank, m // 2 // chips), bf16),
            pltpu.VMEM((rank, m // 2 // chips), bf16),
            pltpu.SemaphoreType.DMA((4,)),
            pltpu.SemaphoreType.DMA((own // PIECE,)),
            pltpu.SemaphoreType.DMA((own // PIECE,)),
            pltpu.SemaphoreType.DMA((copies,)),
            pltpu.SemaphoreType.DMA((copies,)),
        ],
        compiler_params=pltpu.CompilerParams(
            collective_id=0, has_side_effects=True, vmem_limit_bytes=48 * 1024 * 1024
        ),
        name="exchange",
    )(*(pltpu.with_memory_space_constraint(a, pltpu.HBM) for a in (inputs.T, grad_out, error, q_prev.T)))

    new_error, basis, q_own = pl.pallas_call(
        store_kernel,
        out_shape=(
            jax.ShapeDtypeStruct(error.shape, bf16),
            jax.ShapeDtypeStruct((rank, n), f32),
            jax.ShapeDtypeStruct((rank, own), f32),
        ),
        in_specs=[vmem] * 3,
        out_specs=(anywhere,) * 3,
        scratch_shapes=[pltpu.SemaphoreType.DMA((8 + 2,))],
        compiler_params=pltpu.CompilerParams(vmem_limit_bytes=4 * 1024 * 1024),
        name="store",
    )(*results)
    return new_error, basis.T, q_own.T


def general_form(inputs, grad_out, error, q_prev):
    highest = lax.Precision.HIGHEST
    replicas = lax.axis_size("dp")
    shards = lax.axis_size("mp")
    own_rows = grad_out.shape[1]
    rank = q_prev.shape[1]
    q_full = lax.all_gather(q_prev, "mp", axis=0, tiled=True)
    prod = lax.dot_general(
        grad_out,
        lax.all_gather(inputs, "mp", axis=1, tiled=True),
        (((0,), (0,)), ((), ())),
        preferred_element_type=jnp.float32,
    )
    merged = prod + error.astype(jnp.float32)
    local_p = jnp.dot(merged, q_full, precision=highest)
    factor = lax.psum(local_p, "dp") / replicas
    gram = lax.psum(jnp.dot(factor.T, factor, precision=highest), "mp")
    ridge = 0.01 * jnp.trace(gram) / rank + 1e-06
    gram = gram + ridge * jnp.eye(rank, dtype=jnp.float32)
    lower = jnp.linalg.cholesky(gram)
    p_hat = jax.scipy.linalg.solve_triangular(lower, factor.T, lower=True).T
    q_term = lax.dot_general(merged, p_hat, (((0,), (0,)), ((), ())), precision=highest)
    q_part = lax.psum_scatter(
        q_term.astype(jnp.bfloat16), "mp", scatter_dimension=0, tiled=True
    ).astype(jnp.float32)
    q_own = lax.psum(q_part, "dp") / replicas
    q_whole = lax.all_gather(q_own.astype(jnp.bfloat16), "mp", axis=0, tiled=True).astype(
        q_own.dtype
    )
    approx = jnp.dot(p_hat, q_whole.T, precision=highest)
    new_error = (merged - approx).astype(jnp.bfloat16)
    scale = jnp.sqrt(jnp.float32(own_rows * shards))
    return (new_error, p_hat * scale, q_own)


def solution(mesh):
    paired = mesh.shape["mp"] == 2 and mesh.shape["dp"] % 4 == 0 and mesh.shape["dp"] > 4
    return jax.shard_map(
        per_device if paired else general_form,
        mesh=mesh,
        in_specs=(P("dp", "mp"), P("dp", "mp"), P(("dp", "mp"), None), P("mp", None)),
        out_specs=(P(("dp", "mp"), None), P("mp", None), P("mp", None)),
        check_vma=False,
    )
```

```python
import functools

import jax
import jax.numpy as jnp
from jax import lax
from jax.experimental import pallas as pl
from jax.experimental.pallas import tpu as pltpu
from jax.sharding import PartitionSpec as P

MESH = pl.DeviceIdType.MESH
PIECE = 64
NN = (((1,), (0,)), ((), ()))
NT = (((1,), (1,)), ((), ()))
TN = (((0,), (0,)), ((), ()))
TT = (((0,), (1,)), ((), ()))
LANES = 128


def dot(a, b, dims=NN):
    return lax.dot_general(a, b, dims, preferred_element_type=jnp.float32)


def exact(a, b, dims=NN):
    return lax.dot_general(a, b, dims, precision=lax.Precision.HIGHEST, preferred_element_type=jnp.float32)


def split(value):
    head = value.astype(jnp.bfloat16)
    rest = (value - head.astype(jnp.float32)).astype(jnp.bfloat16)
    return jnp.concatenate([head, rest], axis=0)


def fold(terms):
    rank = terms.shape[0] // 2
    return terms[:rank] + terms[rank:]


def inverse_factor(gram):
    rank = gram.shape[0]
    row = lax.broadcasted_iota(jnp.int32, gram.shape, 0)
    diag = row == lax.broadcasted_iota(jnp.int32, gram.shape, 1)
    ridge = 0.01 * jnp.sum(jnp.where(diag, gram, 0.0), keepdims=True) / rank + 1e-06
    work = jnp.concatenate([gram + jnp.where(diag, ridge, 0.0), jnp.where(diag, 1.0, 0.0)], axis=1)
    wide = 2 * rank
    blocks = [work[i : i + 8] for i in range(0, rank, 8)]
    row8 = lax.broadcasted_iota(jnp.int32, (8, wide), 0)
    per = 8
    for k in range(0, rank, per):
        first = k // 8
        live = range(first, rank // 8)
        cols = [{i: jnp.broadcast_to(blocks[i][:, j : j + 1], (8, wide)) for i in live} for j in range(k, k + per)]
        at = k % 8
        rows = [blocks[first][at + j : at + j + 1] for j in range(per)]
        for s in range(0, per, 2):
            def pick(j, i):
                return cols[j][first][at + i : at + i + 1]
            a, b, c = pick(s, s), pick(s + 1, s), pick(s + 1, s + 1)
            ra, rdet = 1.0 / a, 1.0 / (a * c - b * b)
            ratio = b * ra
            follow = rows[s + 1] - ratio * rows[s]
            scale = a * rdet
            f0, f1 = {}, {}
            for i in live:
                x = cols[s][i] * ra
                if i == first:
                    x = jnp.where(row8 > at + s, x, 0.0)
                y = (cols[s + 1][i] - x * b) * scale
                if i == first:
                    y = jnp.where(row8 > at + s + 1, y, 0.0)
                f0[i], f1[i] = x, y
            for j in range(s + 2, per):
                top = pick(j, s)
                low = pick(j, s + 1) - ratio * top
                cols[j] = {i: cols[j][i] - f0[i] * top - f1[i] * low for i in live}
                here = slice(at + j, at + j + 1)
                rows[j] = rows[j] - f0[first][here] * rows[s] - f1[first][here] * follow
            for i in live:
                blocks[i] = blocks[i] - f0[i] * rows[s] - f1[i] * follow
    work = jnp.concatenate(blocks, axis=0)
    pivots = jnp.sum(jnp.where(diag, work[:, :rank], 0.0), axis=1, keepdims=True)
    return work[:, rank:] * lax.rsqrt(pivots)


def apply(factor, value):
    head = factor.astype(jnp.bfloat16)
    rest = (factor - head.astype(jnp.float32)).astype(jnp.bfloat16)
    pair = split(value)
    return dot(jnp.concatenate([head, head, rest], axis=1), jnp.concatenate([pair, pair[: value.shape[0]]], axis=0))


def exchange_kernel(
    n_dp, x_hbm, g_hbm, e_hbm, q_hbm,
    out_ref, basis_ref, qown_ref,
    merged_ref, pair_ref, qg_ref, g_ref, q_ref, e_ref, xf, qs, u_send, u_recv, v_send, v_recv, pw, p1, p2, pg, gs, qf, xt, q1, qb, q2, y1, y2,
    load_sem, x_ssem, x_rsem, ssem, rsem,
):
    dp, mp = lax.axis_index("dp"), lax.axis_index("mp")
    core, xx, zz = lax.rem(dp, 2), lax.rem(dp // 2, 2), dp // 4
    n_z = n_dp // 4
    chips = n_dp // 2
    rank, own = q_ref.shape
    n, features = merged_ref.shape
    m = qf.shape[1]

    def device(d_core, d_x, d_y, k):
        z = lax.rem(zz + k, n_z)
        c = 1 - core if d_core else core
        x = 1 - xx if d_x else xx
        return ((z * 2 + x) * 2 + c, 1 - mp if d_y else mp)

    core_mate, y_mate = device(1, 0, 0, 0), device(0, 0, 1, 0)
    offsets = [(a, k) for a in (1, 0) for k in range(n_z) if (a, k) != (0, 0)]
    peers = [device(0, a, 0, k) for a, k in offsets]
    places = [(1 - xx if a else xx) * n_z + lax.rem(zz + k, n_z) for a, k in offsets]
    origins = [(1 - xx if a else xx) * n_z + lax.rem(zz + n_z - k, n_z) for a, k in offsets]
    place = xx * n_z + zz
    near = 1 - 2 * lax.rem(zz, 2) + n_z
    squad = [device(0, 1, 0, 0), device(0, 0, 0, near), device(0, 1, 0, near)]

    x_base = pl.multiple_of(mp * own, PIECE)
    mine = pl.ds(x_base, own)
    load_x = pltpu.make_async_copy(x_hbm, xf.at[mine], load_sem.at[0])
    load_e = pltpu.make_async_copy(e_hbm, e_ref, load_sem.at[1])
    load_g = pltpu.make_async_copy(g_hbm, g_ref, load_sem.at[2])
    load_q = pltpu.make_async_copy(q_hbm, q_ref, load_sem.at[3])
    load_q.start()
    load_x.start()
    barrier = pltpu.get_barrier_semaphore()
    mates = [core_mate, y_mate] + peers
    for mate in mates:
        pl.semaphore_signal(barrier, inc=1, device_id=mate, device_id_type=MESH)

    sent = []

    def send(src, dst, mate):
        index = len(sent)
        copy = pltpu.make_async_remote_copy(
            src_ref=src, dst_ref=dst, send_sem=ssem.at[index], recv_sem=rsem.at[index],
            device_id=mate, device_id_type=MESH,
        )
        copy.start()
        sent.append(copy)
        return copy

    pieces = own // PIECE
    flat = own // LANES * LANES
    middle = pl.multiple_of(mp * own + (1 - mp) * flat, PIECE)
    flying, started, landed = [], [0], [0]

    def start_part(row, size):
        part = pl.ds(pl.multiple_of(row, PIECE), size)
        copy = pltpu.make_async_remote_copy(
            src_ref=xf.at[part], dst_ref=xf.at[part],
            send_sem=x_ssem.at[len(flying)], recv_sem=x_rsem.at[len(flying)],
            device_id=y_mate, device_id_type=MESH,
        )
        copy.start()
        flying.append((started[0] + size // PIECE, copy))
        started[0] += size // PIECE

    def start_x(count):
        count = min(count, pieces - 1 - started[0])
        if count > 0:
            start_part(x_base + (mp + started[0]) * PIECE, count * PIECE)

    def land_x(count):
        while landed[0] < len(flying) and (landed[0] == 0 or flying[landed[0] - 1][0] < count):
            flying[landed[0]][1].wait_recv()
            landed[0] += 1

    def merge(begin, size):
        columns = pl.ds(pl.multiple_of(begin, LANES), size)
        product = dot(g_ref[...], xf[columns, :], TT)
        merged_ref[:, columns] = product + e_ref[:, columns].astype(jnp.float32)

    def merge_own(step):
        size = flat // 3
        merge(mp * (flat + LANES) + step * size, size)

    def merge_other(begin, end):
        land_x(end // PIECE)
        merge((1 - mp) * (flat + LANES) + begin, end - begin)

    load_q.wait()
    q_own = q_ref[...]
    edge = qs.shape[2] - own
    shifted = pltpu.roll(jnp.concatenate([q_own, jnp.zeros((rank, edge), jnp.float32)], axis=1), mp * edge, 1)
    qs[mp] = split(shifted)
    load_x.wait()
    load_g.start()
    load_e.start()
    u_own = fold(dot(split(q_own), xf[mine]))
    u_send[...] = u_own
    pl.semaphore_wait(barrier, len(mates))
    corner = xx * 2 + lax.rem(zz, 2)
    side = qs.shape[2] // 2
    piece = side // 4

    def q_part(where):
        return (slice(None), pl.ds(pl.multiple_of(core * side + where * piece, piece), piece))

    q_copy = send(qs.at[(mp, *q_part(corner))], qs.at[(mp, *q_part(corner))], y_mate)
    u_copy = send(u_send, u_recv, y_mate)
    start_x(STEPS[0])
    load_g.wait()
    load_e.wait()

    def e_q(half, begin, width, rows):
        columns = pl.ds(pl.multiple_of(begin, LANES), width)
        wide = pl.ds(pl.multiple_of(half * (features - qs.shape[2]) + begin, LANES), width)
        return fold(dot(qs[half, :, columns], e_ref[rows, wide], NT))

    pw[...] = e_q(mp, 0, 2 * side, slice(None))
    q_copy.wait_recv()
    theirs = 1 - mp
    copies = [send(qs.at[(theirs, *q_part(corner))], qs.at[(theirs, *q_part(corner))], mate) for mate in squad]
    q_pass = [send(qs.at[(theirs, *q_part(corner))], qs.at[(theirs, *q_part(corner))], core_mate)]
    start_x(STEPS[8])
    merge_own(0)
    u_copy.wait_recv()
    pw[...] = pw[...] + fold(dot(split(u_own + u_recv[...]), g_ref[...]))
    corners = [corner + 2 - 4 * xx, corner + 1 - 2 * lax.rem(zz, 2), 3 - corner]
    for copy, where in zip(copies, corners):
        copy.wait_recv()
        q_pass.append(send(qs.at[(theirs, *q_part(where))], qs.at[(theirs, *q_part(where))], core_mate))
    pw[...] = pw[...] + e_q(theirs, core * side, side, slice(None))
    for copy in q_pass:
        copy.wait_recv()

    def part(offset, size):
        return pl.ds(pl.multiple_of(offset, size), size)

    n1, height = n // 2, rank // chips
    b1 = part(core * n1, n1)
    level = part(place * height, height)
    away = part((1 - core) * n1, n1)
    pw[:, away] = pw[:, away] + e_q(theirs, (1 - core) * side, side, away)
    copy = send(pw.at[:, away], p1, core_mate)
    start_x(STEPS[1])
    pw[:, b1] = pw[:, b1] + e_q(theirs, (1 - core) * side, side, b1)
    copy.wait_recv()
    pw[:, b1] = pw[:, b1] + p1[...]
    copies = [
        send(pw.at[part(there * height, height), b1], p2.at[k], mate)
        for k, (there, mate) in enumerate(zip(places, peers))
    ]
    start_x(STEPS[2])
    merge_own(1)
    total = pw[level, b1]
    for k, copy in enumerate(copies):
        copy.wait_recv()
        total = total + p2[k]
    pg[level, b1] = total * (1.0 / n_dp)
    copies = [send(pg.at[level, b1], pg.at[level, b1], mate) for mate in peers]
    p_pass = [send(pg.at[level, b1], pg.at[level, b1], core_mate)]
    start_x(STEPS[3])
    merge_own(2)
    for copy, there in zip(copies, origins):
        copy.wait_recv()
        block = part(there * height, height)
        p_pass.append(send(pg.at[block, b1], pg.at[block, b1], core_mate))

    p_half = pg[:, b1]
    slot = mp * 2 + core
    gs[slot] = exact(p_half, p_half, NT)
    grams = [send(gs.at[slot], gs.at[slot], mate) for mate in (y_mate, core_mate)]
    for copy in p_pass:
        copy.wait_recv()
    mean = pg[...]
    mean_pair = split(mean)
    v_own = fold(dot(mean_pair, g_ref[...], NT))
    v_send[...] = v_own
    v_copy = send(v_send, v_recv, y_mate)
    start_x(STEPS[4])
    qf[:, features:] = jnp.zeros((rank, m - features), jnp.float32)
    for lo in range(0, features, m // 4):
        hi = min(lo + m // 4, features)
        qf[:, lo:hi] = fold(dot(mean_pair, e_ref[:, lo:hi]))
    grams[0].wait_recv()
    grams[0] = send(gs.at[slot + 2 - 4 * mp], gs.at[slot + 2 - 4 * mp], core_mate)
    for copy in grams:
        copy.wait_recv()
    lower = inverse_factor(gs[0] + gs[1] + gs[2] + gs[3])

    v_copy.wait_recv()
    xt[:, own:] = jnp.zeros((rank, xt.shape[1] - own), jnp.float32)
    xt[:, :own] = fold(dot(split(v_own + v_recv[...]), xf[mine], NT))
    m1, m2 = m // 2, m // 2 // chips

    @pl.when(mp == 0)
    def _():
        qf[:, :m1] = qf[:, :m1] + xt[...]

    @pl.when(mp == 1)
    def _():
        qf[:, features - m1 : features] = qf[:, features - m1 : features] + pltpu.roll(xt[...], m1 - own, 1)

    a2 = part(core * m1 + place * m2, m2)
    m3 = m1 // 2
    groups = (1 - xx, xx)
    halves = [send(qf.at[:, part((1 - core) * m1 + there * m3, m3)], q1.at[:, part(there * m3, m3)], core_mate) for there in groups]
    start_x(STEPS[5])
    p_hat = exact(lower, mean)
    basis_ref[...] = p_hat * jnp.sqrt(jnp.float32(n * lax.axis_size("mp")))
    pair_ref[...] = split(p_hat).T
    copies = []
    for copy, there in zip(halves, groups):
        copy.wait_recv()
        columns = part(there * m3, m3)
        value = apply(lower, (qf[:, part(core * m1 + there * m3, m3)] + q1[:, columns]) * (1.0 / n_dp))
        q1[:, columns] = value
        qb[:, columns] = value.astype(jnp.bfloat16)
        for k in range(len(copies), n_z if there is groups[0] else chips - 1):
            copies.append(send(qb.at[:, part(places[k] * m2, m2)], q2.at[k], peers[k]))
    start_x(STEPS[6])
    merge_other(0, flat // 3)
    total = q1[:, part(place * m2, m2)]
    for k, copy in enumerate(copies):
        copy.wait_recv()
        total = total + q2[k].astype(jnp.float32)
    y1[...] = total.astype(jnp.bfloat16)
    copy = send(y1, y2, y_mate)
    start_x(STEPS[7])
    copy.wait_recv()
    qg_ref[:, a2] = (total + y2[...].astype(jnp.float32)).astype(jnp.bfloat16)
    copies = [send(qg_ref.at[:, a2], qg_ref.at[:, a2], mate) for mate in peers]
    q_pass = [send(qg_ref.at[:, a2], qg_ref.at[:, a2], core_mate)]
    for _ in range(4):
        start_x(-(-(pieces - 1 - started[0]) // 2))
    start_x(pieces)
    start_part(middle, PIECE)
    third, far = flat // 3, flat + LANES

    def finish(begin, size):
        columns = pl.ds(pl.multiple_of(begin, LANES), size)
        factor = qg_ref[:, columns]
        approx = dot(pair_ref[...], jnp.concatenate([factor, factor], axis=0))
        out_ref[:, columns] = (merged_ref[:, columns] - approx).astype(jnp.bfloat16)

    merge_other(third, 2 * third)
    for copy, there in zip(copies, origins):
        copy.wait_recv()
        columns = part(core * m1 + there * m2, m2)
        q_pass.append(send(qg_ref.at[:, columns], qg_ref.at[:, columns], core_mate))

    def finish_own():
        for step in range(3):
            finish(mp * far + step * third, third)

    def finish_other():
        for step in range(2):
            finish((1 - mp) * far + step * third, third)

    pl.when(core == mp)(finish_own)
    pl.when(core != mp)(finish_other)
    for copy in q_pass:
        copy.wait_recv()
    pl.when(core != mp)(finish_own)
    pl.when(core == mp)(finish_other)

    @pl.when(mp == 0)
    def _():
        qown_ref[...] = qg_ref[:, :own].astype(jnp.float32)

    @pl.when(mp == 1)
    def _():
        late = qg_ref[:, flat:features].astype(jnp.float32)
        qown_ref[...] = pltpu.roll(late, own, 1)[:, :own]

    for begin, end in ((2 * third, 2 * third + 3 * LANES), (2 * third + 3 * LANES, flat)):
        merge_other(begin, end)
        finish((1 - mp) * far + begin, end - begin)
    land_x(pieces)
    merge(flat, LANES)
    finish(flat, LANES)
    for copy in sent + [copy for _, copy in flying]:
        copy.wait_send()


STEPS = (2, 1, 3, 3, 3, 1, 4, 2, 4)


def store_kernel(*refs):
    sources, targets, sems = refs[:3], refs[3:6], refs[6]
    blocks = sems.shape[0] - 2
    size = sources[0].shape[0] // blocks
    copies = []
    for k in range(blocks):
        rows = pl.ds(k * size, size)
        copies.append(pltpu.make_async_copy(sources[0].at[rows], targets[0].at[rows], sems.at[k]))
    for k in (1, 2):
        copies.append(pltpu.make_async_copy(sources[k], targets[k], sems.at[blocks + k - 1]))
    for copy in copies:
        copy.start()
    for copy in copies:
        copy.wait()


def per_device(inputs, grad_out, error, q_prev):
    n_dp = lax.axis_size("dp")
    chips = n_dp // 2
    tokens, own = inputs.shape
    n, features = error.shape
    rank = q_prev.shape[1]
    m = -(-features // 1024) * 1024
    even = features == 2 * own and own % LANES == PIECE and m == 2 * (own + PIECE) and own // LANES % 15 == 0
    if not even or rank % (8 * chips) or m % (256 * chips) or tokens % LANES or n % 256:
        return general_form(inputs, grad_out, error, q_prev)
    f32, bf16 = jnp.float32, jnp.bfloat16
    vmem, anywhere = pl.BlockSpec(memory_space=pltpu.VMEM), pl.BlockSpec(memory_space=pl.ANY)
    copies = 10 + 3 * chips + 4 + 2 + 3 * chips
    results = pl.pallas_call(
        functools.partial(exchange_kernel, n_dp),
        out_shape=(
            pltpu.VMEM((n, features), bf16),
            pltpu.VMEM((rank, n), f32),
            pltpu.VMEM((rank, own), f32),
        ),
        in_specs=[pl.BlockSpec(memory_space=pltpu.HBM)] * 4,
        out_specs=(vmem,) * 3,
        scratch_shapes=[
            pltpu.VMEM((n, features), f32),
            pltpu.VMEM((n, 2 * rank), bf16),
            pltpu.VMEM((rank, m), bf16),
            pltpu.VMEM((tokens, n), bf16),
            pltpu.VMEM((rank, own), f32),
            pltpu.VMEM((n, features), bf16),
            pltpu.VMEM((features, tokens), bf16),
            pltpu.VMEM((2, 2 * rank, -(-own // LANES) * LANES), bf16),
            pltpu.VMEM((rank, tokens), f32),
            pltpu.VMEM((rank, tokens), f32),
            pltpu.VMEM((rank, tokens), f32),
            pltpu.VMEM((rank, tokens), f32),
            pltpu.VMEM((rank, n), f32),
            pltpu.VMEM((rank, n // 2), f32),
            pltpu.VMEM((chips - 1, rank // chips, n // 2), f32),
            pltpu.VMEM((rank, n), f32),
            pltpu.VMEM((4, rank, rank), f32),
            pltpu.VMEM((rank, m), f32),
            pltpu.VMEM((rank, m // 2), f32),
            pltpu.VMEM((rank, m // 2), f32),
            pltpu.VMEM((rank, m // 2), bf16),
            pltpu.VMEM((chips - 1, rank, m // 2 // chips), bf16),
            pltpu.VMEM((rank, m // 2 // chips), bf16),
            pltpu.VMEM((rank, m // 2 // chips), bf16),
            pltpu.SemaphoreType.DMA((4,)),
            pltpu.SemaphoreType.DMA((own // PIECE,)),
            pltpu.SemaphoreType.DMA((own // PIECE,)),
            pltpu.SemaphoreType.DMA((copies,)),
            pltpu.SemaphoreType.DMA((copies,)),
        ],
        compiler_params=pltpu.CompilerParams(
            collective_id=0, has_side_effects=True, vmem_limit_bytes=48 * 1024 * 1024
        ),
        name="exchange",
    )(*(pltpu.with_memory_space_constraint(a, pltpu.HBM) for a in (inputs.T, grad_out, error, q_prev.T)))

    new_error, basis, q_own = pl.pallas_call(
        store_kernel,
        out_shape=(
            jax.ShapeDtypeStruct(error.shape, bf16),
            jax.ShapeDtypeStruct((rank, n), f32),
            jax.ShapeDtypeStruct((rank, own), f32),
        ),
        in_specs=[vmem] * 3,
        out_specs=(anywhere,) * 3,
        scratch_shapes=[pltpu.SemaphoreType.DMA((8 + 2,))],
        compiler_params=pltpu.CompilerParams(vmem_limit_bytes=4 * 1024 * 1024),
        name="store",
    )(*results)
    return new_error, basis.T, q_own.T


def general_form(inputs, grad_out, error, q_prev):
    highest = lax.Precision.HIGHEST
    replicas = lax.axis_size("dp")
    shards = lax.axis_size("mp")
    own_rows = grad_out.shape[1]
    rank = q_prev.shape[1]
    q_full = lax.all_gather(q_prev, "mp", axis=0, tiled=True)
    prod = lax.dot_general(
        grad_out,
        lax.all_gather(inputs, "mp", axis=1, tiled=True),
        (((0,), (0,)), ((), ())),
        preferred_element_type=jnp.float32,
    )
    merged = prod + error.astype(jnp.float32)
    local_p = jnp.dot(merged, q_full, precision=highest)
    factor = lax.psum(local_p, "dp") / replicas
    gram = lax.psum(jnp.dot(factor.T, factor, precision=highest), "mp")
    ridge = 0.01 * jnp.trace(gram) / rank + 1e-06
    gram = gram + ridge * jnp.eye(rank, dtype=jnp.float32)
    lower = jnp.linalg.cholesky(gram)
    p_hat = jax.scipy.linalg.solve_triangular(lower, factor.T, lower=True).T
    q_term = lax.dot_general(merged, p_hat, (((0,), (0,)), ((), ())), precision=highest)
    q_part = lax.psum_scatter(
        q_term.astype(jnp.bfloat16), "mp", scatter_dimension=0, tiled=True
    ).astype(jnp.float32)
    q_own = lax.psum(q_part, "dp") / replicas
    q_whole = lax.all_gather(q_own.astype(jnp.bfloat16), "mp", axis=0, tiled=True).astype(
        q_own.dtype
    )
    approx = jnp.dot(p_hat, q_whole.T, precision=highest)
    new_error = (merged - approx).astype(jnp.bfloat16)
    scale = jnp.sqrt(jnp.float32(own_rows * shards))
    return (new_error, p_hat * scale, q_own)


def solution(mesh):
    paired = mesh.shape["mp"] == 2 and mesh.shape["dp"] % 4 == 0 and mesh.shape["dp"] > 4
    return jax.shard_map(
        per_device if paired else general_form,
        mesh=mesh,
        in_specs=(P("dp", "mp"), P("dp", "mp"), P(("dp", "mp"), None), P("mp", None)),
        out_specs=(P(("dp", "mp"), None), P("mp", None), P("mp", None)),
        check_vma=False,
    )
```

```python
import functools

import jax
import jax.numpy as jnp
from jax import lax
from jax.experimental import pallas as pl
from jax.experimental.pallas import tpu as pltpu
from jax.sharding import PartitionSpec as P

MESH = pl.DeviceIdType.MESH
PIECE = 64
NN = (((1,), (0,)), ((), ()))
NT = (((1,), (1,)), ((), ()))
TN = (((0,), (0,)), ((), ()))
TT = (((0,), (1,)), ((), ()))
LANES = 128


def dot(a, b, dims=NN):
    return lax.dot_general(a, b, dims, preferred_element_type=jnp.float32)


def exact(a, b, dims=NN):
    return lax.dot_general(a, b, dims, precision=lax.Precision.HIGHEST, preferred_element_type=jnp.float32)


def split(value):
    head = value.astype(jnp.bfloat16)
    rest = (value - head.astype(jnp.float32)).astype(jnp.bfloat16)
    return jnp.concatenate([head, rest], axis=0)


def fold(terms):
    rank = terms.shape[0] // 2
    return terms[:rank] + terms[rank:]


def inverse_factor(gram):
    rank = gram.shape[0]
    row = lax.broadcasted_iota(jnp.int32, gram.shape, 0)
    diag = row == lax.broadcasted_iota(jnp.int32, gram.shape, 1)
    ridge = 0.01 * jnp.sum(jnp.where(diag, gram, 0.0), keepdims=True) / rank + 1e-06
    work = jnp.concatenate([gram + jnp.where(diag, ridge, 0.0), jnp.where(diag, 1.0, 0.0)], axis=1)
    wide = 2 * rank
    blocks = [work[i : i + 8] for i in range(0, rank, 8)]
    row8 = lax.broadcasted_iota(jnp.int32, (8, wide), 0)
    per = 8
    for k in range(0, rank, per):
        first = k // 8
        live = range(first, rank // 8)
        cols = [{i: jnp.broadcast_to(blocks[i][:, j : j + 1], (8, wide)) for i in live} for j in range(k, k + per)]
        at = k % 8
        rows = [blocks[first][at + j : at + j + 1] for j in range(per)]
        for s in range(0, per, 2):
            def pick(j, i):
                return cols[j][first][at + i : at + i + 1]
            a, b, c = pick(s, s), pick(s + 1, s), pick(s + 1, s + 1)
            ra, rdet = 1.0 / a, 1.0 / (a * c - b * b)
            ratio = b * ra
            follow = rows[s + 1] - ratio * rows[s]
            scale = a * rdet
            f0, f1 = {}, {}
            for i in live:
                x = cols[s][i] * ra
                if i == first:
                    x = jnp.where(row8 > at + s, x, 0.0)
                y = (cols[s + 1][i] - x * b) * scale
                if i == first:
                    y = jnp.where(row8 > at + s + 1, y, 0.0)
                f0[i], f1[i] = x, y
            for j in range(s + 2, per):
                top = pick(j, s)
                low = pick(j, s + 1) - ratio * top
                cols[j] = {i: cols[j][i] - f0[i] * top - f1[i] * low for i in live}
                here = slice(at + j, at + j + 1)
                rows[j] = rows[j] - f0[first][here] * rows[s] - f1[first][here] * follow
            for i in live:
                blocks[i] = blocks[i] - f0[i] * rows[s] - f1[i] * follow
    work = jnp.concatenate(blocks, axis=0)
    pivots = jnp.sum(jnp.where(diag, work[:, :rank], 0.0), axis=1, keepdims=True)
    return work[:, rank:] * lax.rsqrt(pivots)


def apply(factor, value):
    head = factor.astype(jnp.bfloat16)
    rest = (factor - head.astype(jnp.float32)).astype(jnp.bfloat16)
    pair = split(value)
    return dot(jnp.concatenate([head, head, rest], axis=1), jnp.concatenate([pair, pair[: value.shape[0]]], axis=0))


def exchange_kernel(
    n_dp, x_hbm, g_hbm, e_hbm, q_hbm,
    out_ref, basis_ref, qown_ref,
    merged_ref, pair_ref, qg_ref, g_ref, q_ref, e_ref, xf, qs, u_send, u_recv, v_send, v_recv, pw, p1, p2, pg, gs, qf, xt, q1, qb, q2, y1, y2,
    load_sem, x_ssem, x_rsem, ssem, rsem,
):
    dp, mp = lax.axis_index("dp"), lax.axis_index("mp")
    core, xx, zz = lax.rem(dp, 2), lax.rem(dp // 2, 2), dp // 4
    n_z = n_dp // 4
    chips = n_dp // 2
    rank, own = q_ref.shape
    n, features = merged_ref.shape
    m = qf.shape[1]

    def device(d_core, d_x, d_y, k):
        z = lax.rem(zz + k, n_z)
        c = 1 - core if d_core else core
        x = 1 - xx if d_x else xx
        return ((z * 2 + x) * 2 + c, 1 - mp if d_y else mp)

    core_mate, y_mate = device(1, 0, 0, 0), device(0, 0, 1, 0)
    offsets = [(a, k) for a in (1, 0) for k in range(n_z) if (a, k) != (0, 0)]
    peers = [device(0, a, 0, k) for a, k in offsets]
    places = [(1 - xx if a else xx) * n_z + lax.rem(zz + k, n_z) for a, k in offsets]
    origins = [(1 - xx if a else xx) * n_z + lax.rem(zz + n_z - k, n_z) for a, k in offsets]
    place = xx * n_z + zz
    near = 1 - 2 * lax.rem(zz, 2) + n_z
    squad = [device(0, 1, 0, 0), device(0, 0, 0, near), device(0, 1, 0, near)]

    x_base = pl.multiple_of(mp * own, PIECE)
    mine = pl.ds(x_base, own)
    load_x = pltpu.make_async_copy(x_hbm, xf.at[mine], load_sem.at[0])
    load_e = pltpu.make_async_copy(e_hbm, e_ref, load_sem.at[1])
    load_g = pltpu.make_async_copy(g_hbm, g_ref, load_sem.at[2])
    load_q = pltpu.make_async_copy(q_hbm, q_ref, load_sem.at[3])
    load_q.start()
    load_x.start()
    barrier = pltpu.get_barrier_semaphore()
    mates = [core_mate, y_mate] + peers
    for mate in mates:
        pl.semaphore_signal(barrier, inc=1, device_id=mate, device_id_type=MESH)

    sent = []

    def send(src, dst, mate):
        index = len(sent)
        copy = pltpu.make_async_remote_copy(
            src_ref=src, dst_ref=dst, send_sem=ssem.at[index], recv_sem=rsem.at[index],
            device_id=mate, device_id_type=MESH,
        )
        copy.start()
        sent.append(copy)
        return copy

    pieces = own // PIECE
    flat = own // LANES * LANES
    middle = pl.multiple_of(mp * own + (1 - mp) * flat, PIECE)
    flying, started, landed = [], [0], [0]

    def start_part(row, size):
        part = pl.ds(pl.multiple_of(row, PIECE), size)
        copy = pltpu.make_async_remote_copy(
            src_ref=xf.at[part], dst_ref=xf.at[part],
            send_sem=x_ssem.at[len(flying)], recv_sem=x_rsem.at[len(flying)],
            device_id=y_mate, device_id_type=MESH,
        )
        copy.start()
        flying.append((started[0] + size // PIECE, copy))
        started[0] += size // PIECE

    def start_x(count):
        count = min(count, pieces - 1 - started[0])
        if count > 0:
            start_part(x_base + (mp + started[0]) * PIECE, count * PIECE)

    def land_x(count):
        while landed[0] < len(flying) and (landed[0] == 0 or flying[landed[0] - 1][0] < count):
            flying[landed[0]][1].wait_recv()
            landed[0] += 1

    def merge(begin, size):
        columns = pl.ds(pl.multiple_of(begin, LANES), size)
        product = dot(g_ref[...], xf[columns, :], TT)
        merged_ref[:, columns] = product + e_ref[:, columns].astype(jnp.float32)

    def merge_own(step):
        size = flat // 3
        merge(mp * (flat + LANES) + step * size, size)

    def merge_other(begin, end):
        land_x(end // PIECE)
        merge((1 - mp) * (flat + LANES) + begin, end - begin)

    load_q.wait()
    q_own = q_ref[...]
    edge = qs.shape[2] - own
    shifted = pltpu.roll(jnp.concatenate([q_own, jnp.zeros((rank, edge), jnp.float32)], axis=1), mp * edge, 1)
    qs[mp] = split(shifted)
    load_x.wait()
    load_g.start()
    load_e.start()
    u_own = fold(dot(split(q_own), xf[mine]))
    u_send[...] = u_own
    pl.semaphore_wait(barrier, len(mates))
    corner = xx * 2 + lax.rem(zz, 2)
    side = qs.shape[2] // 2
    piece = side // 4

    def q_part(where):
        return (slice(None), pl.ds(pl.multiple_of(core * side + where * piece, piece), piece))

    q_copy = send(qs.at[(mp, *q_part(corner))], qs.at[(mp, *q_part(corner))], y_mate)
    u_copy = send(u_send, u_recv, y_mate)
    start_x(STEPS[0])
    load_g.wait()
    load_e.wait()

    def e_q(half, begin, width, rows):
        columns = pl.ds(pl.multiple_of(begin, LANES), width)
        wide = pl.ds(pl.multiple_of(half * (features - qs.shape[2]) + begin, LANES), width)
        return fold(dot(qs[half, :, columns], e_ref[rows, wide], NT))

    pw[...] = e_q(mp, 0, 2 * side, slice(None))
    q_copy.wait_recv()
    theirs = 1 - mp
    copies = [send(qs.at[(theirs, *q_part(corner))], qs.at[(theirs, *q_part(corner))], mate) for mate in squad]
    q_pass = [send(qs.at[(theirs, *q_part(corner))], qs.at[(theirs, *q_part(corner))], core_mate)]
    start_x(STEPS[8])
    merge_own(0)
    u_copy.wait_recv()
    pw[...] = pw[...] + fold(dot(split(u_own + u_recv[...]), g_ref[...]))
    corners = [corner + 2 - 4 * xx, corner + 1 - 2 * lax.rem(zz, 2), 3 - corner]
    for copy, where in zip(copies, corners):
        copy.wait_recv()
        q_pass.append(send(qs.at[(theirs, *q_part(where))], qs.at[(theirs, *q_part(where))], core_mate))
    pw[...] = pw[...] + e_q(theirs, core * side, side, slice(None))
    for copy in q_pass:
        copy.wait_recv()

    def part(offset, size):
        return pl.ds(pl.multiple_of(offset, size), size)

    n1, height = n // 2, rank // chips
    b1 = part(core * n1, n1)
    level = part(place * height, height)
    away = part((1 - core) * n1, n1)
    pw[:, away] = pw[:, away] + e_q(theirs, (1 - core) * side, side, away)
    copy = send(pw.at[:, away], p1, core_mate)
    start_x(STEPS[1])
    pw[:, b1] = pw[:, b1] + e_q(theirs, (1 - core) * side, side, b1)
    copy.wait_recv()
    pw[:, b1] = pw[:, b1] + p1[...]
    copies = [
        send(pw.at[part(there * height, height), b1], p2.at[k], mate)
        for k, (there, mate) in enumerate(zip(places, peers))
    ]
    start_x(STEPS[2])
    merge_own(1)
    total = pw[level, b1]
    for k, copy in enumerate(copies):
        copy.wait_recv()
        total = total + p2[k]
    pg[level, b1] = total * (1.0 / n_dp)
    copies = [send(pg.at[level, b1], pg.at[level, b1], mate) for mate in peers]
    p_pass = [send(pg.at[level, b1], pg.at[level, b1], core_mate)]
    start_x(STEPS[3])
    merge_own(2)
    for copy, there in zip(copies, origins):
        copy.wait_recv()
        block = part(there * height, height)
        p_pass.append(send(pg.at[block, b1], pg.at[block, b1], core_mate))

    p_half = pg[:, b1]
    slot = mp * 2 + core
    gs[slot] = exact(p_half, p_half, NT)
    grams = [send(gs.at[slot], gs.at[slot], mate) for mate in (y_mate, core_mate)]
    for copy in p_pass:
        copy.wait_recv()
    mean = pg[...]
    mean_pair = split(mean)
    v_own = fold(dot(mean_pair, g_ref[...], NT))
    v_send[...] = v_own
    v_copy = send(v_send, v_recv, y_mate)
    start_x(STEPS[4])
    qf[:, features:] = jnp.zeros((rank, m - features), jnp.float32)
    for lo in range(0, features, m // 4):
        hi = min(lo + m // 4, features)
        qf[:, lo:hi] = fold(dot(mean_pair, e_ref[:, lo:hi]))
    grams[0].wait_recv()
    grams[0] = send(gs.at[slot + 2 - 4 * mp], gs.at[slot + 2 - 4 * mp], core_mate)
    for copy in grams:
        copy.wait_recv()
    lower = inverse_factor(gs[0] + gs[1] + gs[2] + gs[3])

    v_copy.wait_recv()
    xt[:, own:] = jnp.zeros((rank, xt.shape[1] - own), jnp.float32)
    xt[:, :own] = fold(dot(split(v_own + v_recv[...]), xf[mine], NT))
    m1, m2 = m // 2, m // 2 // chips

    @pl.when(mp == 0)
    def _():
        qf[:, :m1] = qf[:, :m1] + xt[...]

    @pl.when(mp == 1)
    def _():
        qf[:, features - m1 : features] = qf[:, features - m1 : features] + pltpu.roll(xt[...], m1 - own, 1)

    a2 = part(core * m1 + place * m2, m2)
    m3 = m1 // 2
    groups = (1 - xx, xx)
    halves = [send(qf.at[:, part((1 - core) * m1 + there * m3, m3)], q1.at[:, part(there * m3, m3)], core_mate) for there in groups]
    start_x(STEPS[5])
    p_hat = exact(lower, mean)
    basis_ref[...] = p_hat * jnp.sqrt(jnp.float32(n * lax.axis_size("mp")))
    pair_ref[...] = split(p_hat).T
    copies = []
    for copy, there in zip(halves, groups):
        copy.wait_recv()
        columns = part(there * m3, m3)
        value = apply(lower, (qf[:, part(core * m1 + there * m3, m3)] + q1[:, columns]) * (1.0 / n_dp))
        q1[:, columns] = value
        qb[:, columns] = value.astype(jnp.bfloat16)
        for k in range(len(copies), n_z if there is groups[0] else chips - 1):
            copies.append(send(qb.at[:, part(places[k] * m2, m2)], q2.at[k], peers[k]))
    start_x(STEPS[6])
    merge_other(0, flat // 3)
    total = q1[:, part(place * m2, m2)]
    for k, copy in enumerate(copies):
        copy.wait_recv()
        total = total + q2[k].astype(jnp.float32)
    y1[...] = total.astype(jnp.bfloat16)
    copy = send(y1, y2, y_mate)
    start_x(STEPS[7])
    copy.wait_recv()
    qg_ref[:, a2] = (total + y2[...].astype(jnp.float32)).astype(jnp.bfloat16)
    copies = [send(qg_ref.at[:, a2], qg_ref.at[:, a2], mate) for mate in peers]
    q_pass = [send(qg_ref.at[:, a2], qg_ref.at[:, a2], core_mate)]
    for _ in range(4):
        start_x(-(-(pieces - 1 - started[0]) // 2))
    start_x(pieces)
    start_part(middle, PIECE)
    third, far = flat // 3, flat + LANES

    def finish(begin, size):
        columns = pl.ds(pl.multiple_of(begin, LANES), size)
        factor = qg_ref[:, columns]
        approx = dot(pair_ref[...], jnp.concatenate([factor, factor], axis=0))
        out_ref[:, columns] = (merged_ref[:, columns] - approx).astype(jnp.bfloat16)

    merge_other(third, 2 * third)
    for copy, there in zip(copies, origins):
        copy.wait_recv()
        columns = part(core * m1 + there * m2, m2)
        q_pass.append(send(qg_ref.at[:, columns], qg_ref.at[:, columns], core_mate))

    def finish_own():
        for step in range(3):
            finish(mp * far + step * third, third)

    def finish_other():
        for step in range(2):
            finish((1 - mp) * far + step * third, third)

    pl.when(core == mp)(finish_own)
    pl.when(core != mp)(finish_other)
    for copy in q_pass:
        copy.wait_recv()
    pl.when(core != mp)(finish_own)
    pl.when(core == mp)(finish_other)

    @pl.when(mp == 0)
    def _():
        qown_ref[...] = qg_ref[:, :own].astype(jnp.float32)

    @pl.when(mp == 1)
    def _():
        late = qg_ref[:, flat:features].astype(jnp.float32)
        qown_ref[...] = pltpu.roll(late, own, 1)[:, :own]

    for begin, end in ((2 * third, 2 * third + 3 * LANES), (2 * third + 3 * LANES, flat)):
        merge_other(begin, end)
        finish((1 - mp) * far + begin, end - begin)
    land_x(pieces)
    merge(flat, LANES)
    finish(flat, LANES)
    for copy in sent + [copy for _, copy in flying]:
        copy.wait_send()


STEPS = (3, 1, 3, 3, 3, 1, 4, 2, 4)


def store_kernel(*refs):
    sources, targets, sems = refs[:3], refs[3:6], refs[6]
    blocks = sems.shape[0] - 2
    size = sources[0].shape[0] // blocks
    copies = []
    for k in range(blocks):
        rows = pl.ds(k * size, size)
        copies.append(pltpu.make_async_copy(sources[0].at[rows], targets[0].at[rows], sems.at[k]))
    for k in (1, 2):
        copies.append(pltpu.make_async_copy(sources[k], targets[k], sems.at[blocks + k - 1]))
    for copy in copies:
        copy.start()
    for copy in copies:
        copy.wait()


def per_device(inputs, grad_out, error, q_prev):
    n_dp = lax.axis_size("dp")
    chips = n_dp // 2
    tokens, own = inputs.shape
    n, features = error.shape
    rank = q_prev.shape[1]
    m = -(-features // 1024) * 1024
    even = features == 2 * own and own % LANES == PIECE and m == 2 * (own + PIECE) and own // LANES % 15 == 0
    if not even or rank % (8 * chips) or m % (256 * chips) or tokens % LANES or n % 256:
        return general_form(inputs, grad_out, error, q_prev)
    f32, bf16 = jnp.float32, jnp.bfloat16
    vmem, anywhere = pl.BlockSpec(memory_space=pltpu.VMEM), pl.BlockSpec(memory_space=pl.ANY)
    copies = 10 + 3 * chips + 4 + 2 + 3 * chips
    results = pl.pallas_call(
        functools.partial(exchange_kernel, n_dp),
        out_shape=(
            pltpu.VMEM((n, features), bf16),
            pltpu.VMEM((rank, n), f32),
            pltpu.VMEM((rank, own), f32),
        ),
        in_specs=[pl.BlockSpec(memory_space=pltpu.HBM)] * 4,
        out_specs=(vmem,) * 3,
        scratch_shapes=[
            pltpu.VMEM((n, features), f32),
            pltpu.VMEM((n, 2 * rank), bf16),
            pltpu.VMEM((rank, m), bf16),
            pltpu.VMEM((tokens, n), bf16),
            pltpu.VMEM((rank, own), f32),
            pltpu.VMEM((n, features), bf16),
            pltpu.VMEM((features, tokens), bf16),
            pltpu.VMEM((2, 2 * rank, -(-own // LANES) * LANES), bf16),
            pltpu.VMEM((rank, tokens), f32),
            pltpu.VMEM((rank, tokens), f32),
            pltpu.VMEM((rank, tokens), f32),
            pltpu.VMEM((rank, tokens), f32),
            pltpu.VMEM((rank, n), f32),
            pltpu.VMEM((rank, n // 2), f32),
            pltpu.VMEM((chips - 1, rank // chips, n // 2), f32),
            pltpu.VMEM((rank, n), f32),
            pltpu.VMEM((4, rank, rank), f32),
            pltpu.VMEM((rank, m), f32),
            pltpu.VMEM((rank, m // 2), f32),
            pltpu.VMEM((rank, m // 2), f32),
            pltpu.VMEM((rank, m // 2), bf16),
            pltpu.VMEM((chips - 1, rank, m // 2 // chips), bf16),
            pltpu.VMEM((rank, m // 2 // chips), bf16),
            pltpu.VMEM((rank, m // 2 // chips), bf16),
            pltpu.SemaphoreType.DMA((4,)),
            pltpu.SemaphoreType.DMA((own // PIECE,)),
            pltpu.SemaphoreType.DMA((own // PIECE,)),
            pltpu.SemaphoreType.DMA((copies,)),
            pltpu.SemaphoreType.DMA((copies,)),
        ],
        compiler_params=pltpu.CompilerParams(
            collective_id=0, has_side_effects=True, vmem_limit_bytes=48 * 1024 * 1024
        ),
        name="exchange",
    )(*(pltpu.with_memory_space_constraint(a, pltpu.HBM) for a in (inputs.T, grad_out, error, q_prev.T)))

    new_error, basis, q_own = pl.pallas_call(
        store_kernel,
        out_shape=(
            jax.ShapeDtypeStruct(error.shape, bf16),
            jax.ShapeDtypeStruct((rank, n), f32),
            jax.ShapeDtypeStruct((rank, own), f32),
        ),
        in_specs=[vmem] * 3,
        out_specs=(anywhere,) * 3,
        scratch_shapes=[pltpu.SemaphoreType.DMA((8 + 2,))],
        compiler_params=pltpu.CompilerParams(vmem_limit_bytes=4 * 1024 * 1024),
        name="store",
    )(*results)
    return new_error, basis.T, q_own.T


def general_form(inputs, grad_out, error, q_prev):
    highest = lax.Precision.HIGHEST
    replicas = lax.axis_size("dp")
    shards = lax.axis_size("mp")
    own_rows = grad_out.shape[1]
    rank = q_prev.shape[1]
    q_full = lax.all_gather(q_prev, "mp", axis=0, tiled=True)
    prod = lax.dot_general(
        grad_out,
        lax.all_gather(inputs, "mp", axis=1, tiled=True),
        (((0,), (0,)), ((), ())),
        preferred_element_type=jnp.float32,
    )
    merged = prod + error.astype(jnp.float32)
    local_p = jnp.dot(merged, q_full, precision=highest)
    factor = lax.psum(local_p, "dp") / replicas
    gram = lax.psum(jnp.dot(factor.T, factor, precision=highest), "mp")
    ridge = 0.01 * jnp.trace(gram) / rank + 1e-06
    gram = gram + ridge * jnp.eye(rank, dtype=jnp.float32)
    lower = jnp.linalg.cholesky(gram)
    p_hat = jax.scipy.linalg.solve_triangular(lower, factor.T, lower=True).T
    q_term = lax.dot_general(merged, p_hat, (((0,), (0,)), ((), ())), precision=highest)
    q_part = lax.psum_scatter(
        q_term.astype(jnp.bfloat16), "mp", scatter_dimension=0, tiled=True
    ).astype(jnp.float32)
    q_own = lax.psum(q_part, "dp") / replicas
    q_whole = lax.all_gather(q_own.astype(jnp.bfloat16), "mp", axis=0, tiled=True).astype(
        q_own.dtype
    )
    approx = jnp.dot(p_hat, q_whole.T, precision=highest)
    new_error = (merged - approx).astype(jnp.bfloat16)
    scale = jnp.sqrt(jnp.float32(own_rows * shards))
    return (new_error, p_hat * scale, q_own)


def solution(mesh):
    paired = mesh.shape["mp"] == 2 and mesh.shape["dp"] % 4 == 0 and mesh.shape["dp"] > 4
    return jax.shard_map(
        per_device if paired else general_form,
        mesh=mesh,
        in_specs=(P("dp", "mp"), P("dp", "mp"), P(("dp", "mp"), None), P("mp", None)),
        out_specs=(P(("dp", "mp"), None), P("mp", None), P("mp", None)),
        check_vma=False,
    )
```
